512 devices in a mesh: len: 64 (over y, z), wid: 8 (over x, core).
Axes of the slice: x: 4, y: 8, z: 8, core: 2. Of those that a mesh axis runs over, the one named last changes fastest.
Arguments:
- density: float32 [16, 4096, 4096], P(None, 'len', 'wid'), may hold values from 0.05 to 1.5
- len_band: int32 [2, 16], replicated, may hold values from 0 to 21, as said below
- wid_band: int32 [2, 16], replicated, may hold values from 0 to 127, as said below
- len_taps: float32 [16, 8], replicated, may hold values from 0.25 to 4
- wid_taps: float32 [16, 8], replicated, may hold values from 0.25 to 4
- tile_pairs: int32 [64, 3], replicated, may hold values from -1 to 3, as said below
- agg_kern: float32 [4, 64, 64], replicated, as said below
Outputs:
- updated: float32 [16, 4096, 4096], P(None, 'len', 'wid')
The draws below stay inside these ranges and needn't reach their ends.
Inputs may be any that keep to these rules, and one draw needn't show every extreme that they name: `len_band`: offset plus count minus one is at most 21 for every batch; counts run from 1 to 8. `wid_band`: offset plus count minus one is at most 127 for every batch; counts run from 1 to 8. `tile_pairs`: -1 marks an absent pair. `agg_kern`: entries are nonnegative.
All inputs are finite; a program needn't handle non-finite values.
Results may differ from the reference program's by a relative error of at most 0.0003.
Values sent between devices are 32-bit elements; how exact they have to be, the bound alone decides.
No kernel may reach another device: no remote copies, remote signals or barrier semaphores. Data moves between devices by JAX's collectives and lax.ppermute only.
A program may use at most 128 MiB of HBM per device.

```python
import math
import jax
import jax.numpy as jnp
from jax import lax

NL = 4096
NW = 4096
B = 16
KMAX = 8
WBLK = 128
NK = 4
LS = 64
NT = 64


def band_draw(key, reach):
    first, second, third = jax.random.split(key, 3)
    counts = jax.random.randint(first, (B,), 2, KMAX + 1)
    offsets = jax.random.randint(second, (B,), 0, reach + 2 - counts)
    chosen = jax.random.randint(third, (), 0, B)
    batch_index = jnp.arange(B)
    top_batch = batch_index == chosen
    counts = jnp.where(top_batch, 1, counts)
    offsets = jnp.where(top_batch, reach, offsets)
    return jnp.stack([offsets, counts]).astype(jnp.int32)


def draw_len_band(key, part):
    return band_draw(jax.random.fold_in(key, 11), LS // 3)


def draw_wid_band(key, part):
    return band_draw(jax.random.fold_in(key, 23), WBLK - 1)


def draw_tile_pairs(key, part):
    first, second = jax.random.split(jax.random.fold_in(key, 53))
    loose = jax.random.randint(first, (NT, 3), -1, NK)
    firm = jax.random.randint(second, (NT, 3), 0, NK)
    tile_index = jnp.arange(NT)[:, None]
    forced = (tile_index == 1) | (tile_index == 2) | (tile_index == NT - 2) | (tile_index == NT - 1)
    return jnp.where(forced, firm, loose).astype(jnp.int32)


def draw_agg_kern(key, part):
    first, second = jax.random.split(jax.random.fold_in(key, 37))
    diagonal = jax.random.uniform(first, (NK, LS), jnp.float32, 0.2, 0.6)
    spread = jax.random.uniform(second, (NK, LS, LS), jnp.float32, 0.0, 1.0) * (0.6 / LS)
    identity = (jnp.arange(LS)[:, None] == jnp.arange(LS)[None, :]).astype(jnp.float32)
    return (spread + identity[None, :, :] * diagonal[:, :, None]).astype(jnp.float32)


def block_scale(key, dims, cuts, low, top_value):
    def one(axis_at, shards_of):
        draws = jax.random.uniform(jax.random.fold_in(jax.random.fold_in(key, 6), axis_at), (shards_of,), jnp.float32, low / len(cuts), top_value / len(cuts))
        return jnp.repeat(jnp.exp(draws), dims[axis_at] // shards_of).reshape((-1,) + (1,) * (len(dims) - axis_at - 1))

    level = one(*cuts[0])
    for cut in cuts[1:]:
        level = level * one(*cut)
    return level


def setup_inputs(seed: int = 0) -> dict:
    splits = jax.random.split(jax.random.key(seed), 8)
    return {
        "density": jnp.clip(jnp.exp(math.log(1.5) - 3.4011974 * jax.random.uniform(splits[0], (B, NL, NW), jnp.float32) ** block_scale(splits[0], (B, NL, NW), ((1, 64), (2, 8)), -0.2, 0.2)), 0.05, 1.5),
        "len_band": draw_len_band(jax.random.fold_in(splits[7], 71), 0),
        "wid_band": draw_wid_band(jax.random.fold_in(splits[7], 71), 0),
        "len_taps": jnp.clip(jnp.exp(jax.random.uniform(splits[3], (B, KMAX), jnp.float32, math.log(0.25), math.log(4.0))), 0.25, 4.0),
        "wid_taps": jnp.clip(jnp.exp(jax.random.uniform(splits[4], (B, KMAX), jnp.float32, math.log(0.25), math.log(4.0))), 0.25, 4.0),
        "tile_pairs": draw_tile_pairs(jax.random.fold_in(splits[7], 71), 0),
        "agg_kern": draw_agg_kern(jax.random.fold_in(splits[7], 71), 0),
    }


BETA = 0.5


def shift_sum(field, offset, count, taps, along_axis, margin):
    tap_range = jnp.arange(KMAX, dtype=jnp.int32)
    weights = jnp.where(tap_range < count, taps, 0.0)
    scaled = weights / jnp.sum(weights)
    widths = [(0, 0), (0, 0)]
    widths[along_axis] = (margin, 0)
    padded = jnp.pad(field, widths)
    result = jnp.zeros_like(field)
    for tap_index in range(KMAX):
        start = (margin - offset - tap_index).astype(jnp.int32)
        piece = lax.dynamic_slice_in_dim(padded, start, field.shape[along_axis], along_axis)
        result = result + scaled[tap_index] * piece
    return result


def reference(density, len_band, wid_band, len_taps, wid_taps, tile_pairs, agg_kern):
    def one_batch(inputs):
        field, len_off, len_cnt, len_wt, wid_off, wid_cnt, wid_wt = inputs
        grown = shift_sum(field, len_off, len_cnt, len_wt, 0, LS // 3 + KMAX)
        spread = shift_sum(grown, wid_off, wid_cnt, wid_wt, 1, WBLK + KMAX)
        padded = jnp.pad(spread, ((2 * LS, 0), (0, 0)))

        def one_tile(tile):
            start = (tile * LS).astype(jnp.int32)
            stacked = lax.dynamic_slice_in_dim(padded, start, 3 * LS, 0)
            pair_row = tile_pairs[tile]
            kernels = []
            for offset_index in (2, 1, 0):
                kernel_id = pair_row[offset_index]
                kernels.append(agg_kern[jnp.maximum(kernel_id, 0)] * (kernel_id >= 0).astype(jnp.float32))
            kernel = jnp.concatenate(kernels, axis=0)
            rate = jnp.dot(kernel.T, stacked, precision=lax.Precision.HIGHEST)
            own = stacked[2 * LS:]
            return own + BETA * (rate * rate / (1.0 + rate) - own * rate)

        tiles = lax.map(one_tile, jnp.arange(NT, dtype=jnp.int32))
        return tiles.reshape(NL, NW)

    return lax.map(one_batch, (density, len_band[0], len_band[1], len_taps, wid_band[0], wid_band[1], wid_taps))
```

```python
import jax
import jax.numpy as jnp
from jax import lax
from jax.sharding import PartitionSpec as P

WBLK = 128
BETA = 0.5
RING = 8
RIM = 24
HIGHEST = lax.Precision.HIGHEST

FORWARD = ((0, 6), (6, 12))
BACKWARD = ((12, 14), (14, 16))


def tap_scale(band, taps):
    tap_range = jnp.arange(taps.shape[1], dtype=jnp.int32)
    weights = jnp.where(tap_range[None, :] < band[1][:, None], taps, 0.0)
    return weights / jnp.sum(weights, axis=1, keepdims=True)


def band_matrix(band, taps, lead_rows, out_span):
    scaled = tap_scale(band, taps)
    source = jnp.arange(lead_rows + out_span, dtype=jnp.int32)[:, None]
    target = jnp.arange(out_span, dtype=jnp.int32)[None, :]
    distance = (lead_rows + target - source)[None, :, :] - band[0][:, None, None]
    matrix = jnp.zeros(distance.shape, jnp.float32)
    for tap_index in range(taps.shape[1]):
        matrix = matrix + jnp.where(distance == tap_index, scaled[:, tap_index][:, None, None], 0.0)
    return matrix


def width_sweep(extended, matrix):
    batches, rows, columns = extended.shape
    groups = columns // WBLK - 1
    blocked = extended.reshape(batches, rows, groups + 1, WBLK)
    paired = jnp.concatenate([blocked[:, :, :-1], blocked[:, :, 1:]], axis=3)
    moved = jnp.einsum("brni,bij->brnj", paired, matrix, precision=HIGHEST)
    return moved.reshape(batches, rows, groups * WBLK)


def shards(density, len_band, wid_band, len_taps, wid_taps, tile_pairs, agg_kern):
    batches, tile_len, group_width = density.shape
    tiles = lax.axis_size("len")
    groups = lax.axis_size("wid")
    me = lax.axis_index("len")

    def spot(tile, step):
        return tile // RING * RING + (tile + step) % RING

    hop = [(t, (t + 1) % tiles) for t in range(tiles)]
    unhop = [(t, (t - 1) % tiles) for t in range(tiles)]
    back_three = [(t, spot(t, -3)) for t in range(tiles)]
    back_five = [(spot(t, -3), (t + 3) % tiles) for t in range(tiles)]

    edge = lax.ppermute(density[:, :, group_width - WBLK :], "wid", [(s, s + 1) for s in range(groups - 1)])
    wid_matrix = band_matrix(wid_band, wid_taps, WBLK, WBLK)
    band = jnp.swapaxes(band_matrix(len_band, len_taps, RIM, tile_len), 1, 2)
    pair_row = lax.dynamic_slice_in_dim(tile_pairs, me, 1, 0)[0]

    def lay(matrix, below):
        left = (2 - below) * tile_len
        return jnp.pad(matrix, ((0, 0), (0, 0), (left, below * tile_len)))

    rate_op = jnp.zeros((batches, tile_len, RIM + 3 * tile_len), jnp.float32)
    for below in range(3):
        kernel_id = pair_row[below]
        kernel = agg_kern[jnp.maximum(kernel_id, 0)] * (kernel_id >= 0).astype(jnp.float32)
        rate_op = rate_op + lay(jnp.einsum("ml,bmi->bli", kernel, band, precision=HIGHEST), below)
    operator = jnp.concatenate([rate_op, lay(band, 0)], axis=1)
    column = jnp.arange(RIM + 3 * tile_len, dtype=jnp.int32)
    tile_of = me - 2 + (column - RIM) // tile_len
    operator = jnp.where((tile_of >= 0)[None, None, :], operator, 0.0)

    swept = []
    stacks = {}
    for part in FORWARD + BACKWARD:
        lo, hi = part
        extended = jnp.concatenate([edge[lo:hi], density[lo:hi]], axis=2)
        stacks[part] = [width_sweep(extended, wid_matrix[lo:hi])]

    for part in FORWARD:
        own = stacks[part][0]
        one = lax.ppermute(own, "len", hop)
        two = lax.ppermute(one, "len", hop)
        rim = lax.ppermute(two[:, tile_len - RIM :], "len", hop)
        stacks[part] = [rim, two, one, own]
    for part in BACKWARD:
        own = stacks[part][0]
        away = lax.ppermute(own, "len", back_three)
        three = lax.ppermute(away, "len", back_five)
        two = lax.ppermute(three, "len", unhop)
        one = lax.ppermute(two, "len", unhop)
        stacks[part] = [three[:, tile_len - RIM :], two, one, own]

    outs = []
    for part in FORWARD + BACKWARD:
        lo, hi = part
        stack = jnp.concatenate(stacks[part], axis=1)
        both = jnp.einsum("bli,biw->blw", operator[lo:hi], stack, precision=HIGHEST)
        rate, spread = both[:, :tile_len], both[:, tile_len:]
        outs.append(spread + BETA * (rate * rate / (1.0 + rate) - spread * rate))
    return jnp.concatenate(outs, axis=0)


def solution(mesh):
    in_specs = (P(None, "len", "wid"), P(), P(), P(), P(), P(), P())
    out_specs = P(None, "len", "wid")
    return jax.shard_map(shards, mesh=mesh, in_specs=in_specs, out_specs=out_specs, check_vma=False)
```

```python
import functools

import jax
import jax.numpy as jnp
from jax import lax
from jax.experimental import pallas as pl
from jax.experimental.pallas import tpu as pltpu
from jax.sharding import PartitionSpec as P

WBLK = 128
BETA = 0.5
RING = 8
RIM = 24
HIGHEST = lax.Precision.HIGHEST

EARLY = (0, 7)
LATE = (7, 13)
BACK = (13, 16)


def tap_scale(band, taps):
    tap_range = jnp.arange(taps.shape[1], dtype=jnp.int32)
    weights = jnp.where(tap_range[None, :] < band[1][:, None], taps, 0.0)
    return weights / jnp.sum(weights, axis=1, keepdims=True)


def band_matrix(band, taps, lead_rows, out_span):
    scaled = tap_scale(band, taps)
    source = jnp.arange(lead_rows + out_span, dtype=jnp.int32)[:, None]
    target = jnp.arange(out_span, dtype=jnp.int32)[None, :]
    distance = (lead_rows + target - source)[None, :, :] - band[0][:, None, None]
    matrix = jnp.zeros(distance.shape, jnp.float32)
    for tap_index in range(taps.shape[1]):
        matrix = matrix + jnp.where(distance == tap_index, scaled[:, tap_index][:, None, None], 0.0)
    return matrix


def sweep_kernel(first, taps, offset_ref, scale_ref, field_ref, edge_ref, out_ref):
    batch = pl.program_id(0) + first
    offset = offset_ref[batch]
    rows = field_ref.shape[1]
    groups = field_ref.shape[2] // WBLK
    lane = lax.broadcasted_iota(jnp.int32, (rows, WBLK), 1)
    turned = [pltpu.roll(edge_ref[0], offset, 1)]
    for group in range(groups):
        turned.append(pltpu.roll(field_ref[0, :, group * WBLK : (group + 1) * WBLK], offset, 1))
    sums = [None] * groups
    for tap in range(taps):
        if tap:
            turned = [pltpu.roll(piece, 1, 1) for piece in turned]
        scale = scale_ref[batch, tap]
        inside = lane >= offset + tap
        for group in range(groups):
            term = scale * jnp.where(inside, turned[group + 1], turned[group])
            sums[group] = term if tap == 0 else sums[group] + term
    for group in range(groups):
        out_ref[0, :, group * WBLK : (group + 1) * WBLK] = sums[group]


def sweep(field, edge, offsets, scales, part, field_first, edge_first):
    lo, hi = part
    _, rows, width = field.shape
    count = hi - lo
    taps = scales.shape[1]
    return pl.pallas_call(
        functools.partial(sweep_kernel, lo, taps),
        grid_spec=pltpu.PrefetchScalarGridSpec(
            num_scalar_prefetch=2,
            grid=(count,),
            in_specs=[
                pl.BlockSpec((1, rows, width), lambda i, o, s: (i + field_first, 0, 0)),
                pl.BlockSpec((1, rows, WBLK), lambda i, o, s: (i + edge_first, 0, 0)),
            ],
            out_specs=pl.BlockSpec((1, rows, width), lambda i, o, s: (i, 0, 0)),
        ),
        out_shape=jax.ShapeDtypeStruct((count, rows, width), jnp.float32),
        cost_estimate=pl.CostEstimate(
            flops=3 * taps * count * rows * width, bytes_accessed=9 * count * rows * width, transcendentals=0
        ),
        name="sweep",
    )(offsets, scales, field, edge)


def split(value):
    high = value.astype(jnp.bfloat16)
    return high, (value - high.astype(jnp.float32)).astype(jnp.bfloat16)


def finish_kernel(op_ref, own_ref, one_ref, two_ref, rim_ref, *rest):
    out_ref, high_ref, low_ref = rest[-3:]
    rows = own_ref.shape[1]
    at = 0
    for ref in (own_ref, one_ref, two_ref, rim_ref):
        high, low = split(ref[0])
        high_ref[at : at + ref.shape[1]] = high
        low_ref[at : at + ref.shape[1]] = low
        at += ref.shape[1]
    op_high, op_low = split(op_ref[0])
    dot = functools.partial(jnp.dot, preferred_element_type=jnp.float32)
    both = dot(op_high, low_ref[...]) + dot(op_low, high_ref[...]) + dot(op_high, high_ref[...])
    rate, spread = both[:rows], both[rows:]
    out_ref[0] = spread + BETA * (rate * rate / (1.0 + rate) - spread * rate)


def finish(operator, own, one, two, rim, part, total, before):
    lo, hi = part
    count, rows, width = own.shape
    depth = operator.shape[2]
    here = lambda i: (i, 0, 0)
    in_specs = [
        pl.BlockSpec((1, operator.shape[1], depth), lambda i: (i + lo, 0, 0)),
        pl.BlockSpec((1, rows, width), here),
        pl.BlockSpec((1, rows, width), here),
        pl.BlockSpec((1, rows, width), here),
        pl.BlockSpec((1, RIM, width), here),
    ]
    operands = [operator, own, one, two, rim]
    aliases = {}
    if before is not None:
        in_specs.append(pl.BlockSpec(memory_space=pl.ANY))
        operands.append(before)
        aliases = {5: 0}
    return pl.pallas_call(
        finish_kernel,
        grid=(count,),
        in_specs=in_specs,
        out_specs=pl.BlockSpec((1, rows, width), lambda i: (i + lo, 0, 0)),
        out_shape=jax.ShapeDtypeStruct((total, rows, width), jnp.float32),
        scratch_shapes=[pltpu.VMEM((depth, width), jnp.bfloat16)] * 2,
        input_output_aliases=aliases,
        cost_estimate=pl.CostEstimate(
            flops=6 * count * 2 * rows * depth * width, bytes_accessed=20 * count * rows * width, transcendentals=0
        ),
        name="finish",
    )(*operands)


def after(value, *earlier):
    return lax.optimization_barrier((value,) + earlier)[0]


def shards(density, len_band, wid_band, len_taps, wid_taps, tile_pairs, agg_kern):
    batches, tile_len, group_width = density.shape
    tiles = lax.axis_size("len")
    groups = lax.axis_size("wid")
    me = lax.axis_index("len")

    def spot(tile, step):
        return tile // RING * RING + (tile + step) % RING

    hop = functools.partial(lax.ppermute, axis_name="len", perm=[(t, (t + 1) % tiles) for t in range(tiles)])
    unhop = functools.partial(lax.ppermute, axis_name="len", perm=[(t, (t - 1) % tiles) for t in range(tiles)])
    back_three = functools.partial(lax.ppermute, axis_name="len", perm=[(t, spot(t, -3)) for t in range(tiles)])
    back_five = functools.partial(
        lax.ppermute, axis_name="len", perm=[(spot(t, -3), (t + 3) % tiles) for t in range(tiles)]
    )
    side = functools.partial(lax.ppermute, axis_name="wid", perm=[(s, s + 1) for s in range(groups - 1)])

    early_one_raw = hop(density[EARLY[0] : EARLY[1]])
    edge = side(density[:, :, group_width - WBLK :])

    offsets = wid_band[0]
    scales = tap_scale(wid_band, wid_taps)

    back_own = sweep(density, edge, offsets, scales, BACK, BACK[0], BACK[0])
    back_away = back_three(back_own)
    late_own = sweep(density, after(edge, back_own), offsets, scales, LATE, LATE[0], LATE[0])
    late_one = hop(late_own)
    early_one_raw = after(early_one_raw, late_own)

    band = jnp.swapaxes(band_matrix(len_band, len_taps, RIM, tile_len), 1, 2)
    pair_row = lax.dynamic_slice_in_dim(tile_pairs, me, 1, 0)[0]

    def lay(matrix, below):
        low, body = matrix[:, :, :RIM], matrix[:, :, RIM:]
        zero = jnp.zeros_like(body)
        columns = [zero, zero, zero, jnp.zeros_like(low)]
        columns[below] = body
        if below < 2:
            columns[below + 1] = jnp.pad(low, ((0, 0), (0, 0), (tile_len - RIM, 0)))
        else:
            columns[3] = low
        return jnp.concatenate(columns, axis=2)

    rate_op = 0.0
    for below in range(3):
        kernel_id = pair_row[below]
        kernel = agg_kern[jnp.maximum(kernel_id, 0)] * (kernel_id >= 0).astype(jnp.float32)
        rate_op = rate_op + lay(jnp.einsum("ml,bmi->bli", kernel, band, precision=HIGHEST), below)
    operator = jnp.concatenate([rate_op, lay(band, 0)], axis=1)
    column = jnp.arange(RIM + 3 * tile_len, dtype=jnp.int32)
    operator = jnp.where((me >= column // tile_len)[None, None, :], operator, 0.0)

    early_edge = side(early_one_raw[:, :, group_width - WBLK :])
    early_own = sweep(density, edge, offsets, scales, EARLY, EARLY[0], EARLY[0])
    early_one = sweep(early_one_raw, early_edge, offsets, scales, EARLY, 0, 0)
    early_two = hop(early_one)
    late_two = hop(late_one)
    back_three_below = back_five(after(back_away, late_one))
    early_rim = hop(after(early_two[:, tile_len - RIM :], back_away))
    back_two = unhop(after(back_three_below, early_two))
    late_rim = hop(after(late_two[:, tile_len - RIM :], back_three_below))
    back_one = unhop(after(back_two, early_two))

    out = finish(operator, early_own, early_one, early_two, early_rim, EARLY, batches, None)
    out = finish(
        operator, back_own, back_one, back_two, back_three_below[:, tile_len - RIM :], BACK, batches, out
    )
    return finish(operator, late_own, late_one, late_two, late_rim, LATE, batches, out)


def solution(mesh):
    in_specs = (P(None, "len", "wid"), P(), P(), P(), P(), P(), P())
    out_specs = P(None, "len", "wid")
    return jax.shard_map(shards, mesh=mesh, in_specs=in_specs, out_specs=out_specs, check_vma=False)
```

```python
import functools
import jax
import jax.numpy as jnp
from jax import lax
from jax.experimental import pallas as pl
from jax.experimental.pallas import tpu as pltpu
from jax.sharding import PartitionSpec as P

WBLK = 128
BETA = 0.5
RIM = 24
VMEM = 16 << 20
FINCOST = 10000000000
NOCOST = pl.CostEstimate(flops=1, bytes_accessed=1, transcendentals=0)


def sweep_kernel(first, taps, step_rows, offset_ref, scale_ref, field_ref, edge_ref, out_ref):
    batch = pl.program_id(0) + first
    offset = offset_ref[batch]
    rows = field_ref.shape[1]
    groups = field_ref.shape[2] // WBLK
    lane = lax.broadcasted_iota(jnp.int32, (step_rows, WBLK), 1) - offset
    scale = [scale_ref[batch, tap] for tap in range(taps)]
    for row in range(0, rows, step_rows):
        here = slice(row, row + step_rows)
        turned = [pltpu.roll(edge_ref[0, here], offset, 1)]
        for group in range(groups):
            turned.append(pltpu.roll(field_ref[0, here, group * WBLK : (group + 1) * WBLK], offset, 1))
        sums = [None] * groups
        for tap in range(taps):
            if tap:
                turned = [pltpu.roll(piece, 1, 1) for piece in turned]
            inside = lane >= tap
            for group in range(groups):
                term = scale[tap] * jnp.where(inside, turned[group + 1], turned[group])
                sums[group] = term if tap == 0 else sums[group] + term
        for group in range(groups):
            out_ref[0, here, group * WBLK : (group + 1) * WBLK] = sums[group]


def split(value):
    high = value.astype(jnp.bfloat16)
    return high, (value - high.astype(jnp.float32)).astype(jnp.bfloat16)


def sweep_mxu_kernel(first, taps, step_rows, offset_ref, scale_ref, field_ref, edge_ref, out_ref):
    batch = pl.program_id(0) + first
    offset = offset_ref[batch]
    rows = field_ref.shape[1]
    groups = field_ref.shape[2] // WBLK
    source = lax.broadcasted_iota(jnp.int32, (2 * WBLK, WBLK), 0)
    target = lax.broadcasted_iota(jnp.int32, (2 * WBLK, WBLK), 1)
    distance = WBLK + target - source - offset
    matrix = jnp.zeros((2 * WBLK, WBLK), jnp.float32)
    for tap in range(taps):
        matrix = jnp.where(distance == tap, scale_ref[batch, tap], matrix)
    mh, ml = split(matrix)
    pieces = [edge_ref[0]] + [field_ref[0, :, g * WBLK : (g + 1) * WBLK] for g in range(groups)]
    parts = [split(p) for p in pieces]
    hi = jnp.concatenate([jnp.concatenate([parts[g][0], parts[g + 1][0]], axis=1) for g in range(groups)], axis=0)
    lo = jnp.concatenate([jnp.concatenate([parts[g][1], parts[g + 1][1]], axis=1) for g in range(groups)], axis=0)
    dot = functools.partial(jnp.dot, preferred_element_type=jnp.float32)
    both = dot(hi, jnp.concatenate([mh, ml], axis=1))
    res = both[:, :WBLK] + both[:, WBLK:] + dot(lo, mh)
    for group in range(groups):
        out_ref[0, :, group * WBLK : (group + 1) * WBLK] = res[group * rows : (group + 1) * rows]


def sweep(field, edge, offsets, scales, part, field_first, edge_first, kern=sweep_kernel, step_rows=8):
    lo, hi = part
    _, rows, width = field.shape
    count = hi - lo
    taps = scales.shape[1]
    return pl.pallas_call(
        functools.partial(kern, lo, taps, step_rows),
        grid_spec=pltpu.PrefetchScalarGridSpec(
            num_scalar_prefetch=2,
            grid=(count,),
            in_specs=[
                pl.BlockSpec((1, rows, width), lambda i, o, s: (i + field_first, 0, 0)),
                pl.BlockSpec((1, rows, WBLK), lambda i, o, s: (i + edge_first, 0, 0)),
            ],
            out_specs=pl.BlockSpec((1, rows, width), lambda i, o, s: (i, 0, 0)),
        ),
        out_shape=jax.ShapeDtypeStruct((count, rows, width), jnp.float32),
        compiler_params=pltpu.CompilerParams(vmem_limit_bytes=VMEM),
        cost_estimate=NOCOST,
        name="sweep",
    )(offsets, scales, field, edge)


def operator_kernel(taps, spot_ref, offset_ref, scale_ref, own_ref, one_ref, two_ref, out_ref, turn_ref):
    tile_len = own_ref.shape[1]
    batch = pl.program_id(0)
    depth = out_ref.shape[2]

    @pl.when(batch == 0)
    def _():
        for below, ref in enumerate((own_ref, one_ref, two_ref)):
            present = (spot_ref[1 + below] >= 0).astype(jnp.float32)
            turn_ref[:, below * tile_len : (below + 1) * tile_len] = ref[0].T * present

    column = lax.broadcasted_iota(jnp.int32, (3 * tile_len, depth), 1)
    row = lax.broadcasted_iota(jnp.int32, (3 * tile_len, depth), 0)
    tile_row, tile_col = row // tile_len, column // tile_len
    place_row = row % tile_len - tile_len * tile_row
    place_col = column % tile_len - tile_len * tile_col + jnp.where(tile_col == 3, tile_len - RIM, 0)
    distance = jnp.where(spot_ref[0] >= tile_col, place_row - place_col - offset_ref[batch], -1)
    band = jnp.zeros((3 * tile_len, depth), jnp.float32)
    for tap in range(taps):
        band = jnp.where(distance == tap, scale_ref[batch, tap], band)
    band_high, band_low = split(band)
    turn_high, turn_low = split(turn_ref[...])
    dot = functools.partial(jnp.dot, preferred_element_type=jnp.float32)
    rate = dot(turn_high, band_low) + dot(turn_low, band_high) + dot(turn_high, band_high)
    high, low = split(rate)
    out_ref[0, :tile_len] = high
    out_ref[0, tile_len : 2 * tile_len] = band_high[:tile_len]
    out_ref[0, 2 * tile_len : 3 * tile_len] = low
    out_ref[0, 3 * tile_len :] = band_low[:tile_len]


def length_operator(spot, offsets, scales, agg_kern):
    batches, taps = scales.shape
    tile_len = agg_kern.shape[1]
    depth = 3 * tile_len + RIM

    def pick(below):
        return pl.BlockSpec((1, tile_len, tile_len), lambda i, s, o, q: (jnp.maximum(s[1 + below], 0), 0, 0))

    return pl.pallas_call(
        functools.partial(operator_kernel, taps),
        grid_spec=pltpu.PrefetchScalarGridSpec(
            num_scalar_prefetch=3,
            grid=(batches,),
            in_specs=[pick(0), pick(1), pick(2)],
            out_specs=pl.BlockSpec((1, 4 * tile_len, depth), lambda i, s, o, q: (i, 0, 0)),
            scratch_shapes=[pltpu.VMEM((tile_len, 3 * tile_len), jnp.float32)],
        ),
        out_shape=jax.ShapeDtypeStruct((batches, 4 * tile_len, depth), jnp.bfloat16),
        compiler_params=pltpu.CompilerParams(vmem_limit_bytes=VMEM),
        cost_estimate=NOCOST,
        name="operator",
    )(spot, offsets, scales, agg_kern, agg_kern, agg_kern)


def finish_kernel(op_ref, own_ref, one_ref, two_ref, rim_ref, *rest):
    out_ref, high_ref, low_ref = rest[-3:]
    rows = own_ref.shape[1]
    at = 0
    for ref in (own_ref, one_ref, two_ref, rim_ref):
        high, low = split(ref[0])
        high_ref[at : at + ref.shape[1]] = high
        low_ref[at : at + ref.shape[1]] = low
        at += ref.shape[1]
    dot = functools.partial(jnp.dot, preferred_element_type=jnp.float32)
    four = dot(op_ref[0], high_ref[...])
    both = four[: 2 * rows] + four[2 * rows :] + dot(op_ref[0, : 2 * rows], low_ref[...])
    rate, spread = both[:rows], both[rows:]
    out_ref[0] = spread + BETA * (rate * rate / (1.0 + rate) - spread * rate)


def finish(operator, own, one, two, rim, part, total, before, own_first):
    lo, hi = part
    count, rows, width = one.shape
    depth = operator.shape[2]
    here = lambda i: (i, 0, 0)
    in_specs = [
        pl.BlockSpec((1, operator.shape[1], depth), lambda i: (i + lo, 0, 0)),
        pl.BlockSpec((1, rows, width), lambda i: (i + own_first, 0, 0)),
        pl.BlockSpec((1, rows, width), here),
        pl.BlockSpec((1, rows, width), here),
        pl.BlockSpec((1, RIM, width), here),
    ]
    operands = [operator, own, one, two, rim]
    aliases = {}
    if before is not None:
        in_specs.append(pl.BlockSpec(memory_space=pl.ANY))
        operands.append(before)
        aliases = {5: 0}
    return pl.pallas_call(
        finish_kernel,
        grid=(count,),
        in_specs=in_specs,
        out_specs=pl.BlockSpec((1, rows, width), lambda i: (i + lo, 0, 0)),
        out_shape=jax.ShapeDtypeStruct((total, rows, width), jnp.float32),
        scratch_shapes=[pltpu.VMEM((depth, width), jnp.bfloat16)] * 2,
        input_output_aliases=aliases,
        compiler_params=pltpu.CompilerParams(vmem_limit_bytes=VMEM),
        cost_estimate=pl.CostEstimate(flops=FINCOST, bytes_accessed=1, transcendentals=0),
        name="finish",
    )(*operands)


RING = 8
EARLY = (0, 6)
BACK = (6, 9)
LATE = (9, 16)
FIRST = (0, 9)


def tap_scale(band, taps):
    tap_range = jnp.arange(taps.shape[1], dtype=jnp.int32)
    weights = jnp.where(tap_range[None, :] < band[1][:, None], taps, 0.0)
    return weights / jnp.sum(weights, axis=1, keepdims=True)


def after(value, *earlier):
    return lax.optimization_barrier((value,) + earlier)[0]


def shards(density, len_band, wid_band, len_taps, wid_taps, tile_pairs, agg_kern):
    batches, tile_len, group_width = density.shape
    tiles = lax.axis_size("len")
    groups = lax.axis_size("wid")
    me = lax.axis_index("len")
    margin = group_width - WBLK

    def spot(tile, step):
        return tile // RING * RING + (tile + step) % RING

    def move(pairs):
        return functools.partial(lax.ppermute, axis_name="len", perm=pairs)

    hop = move([(t, (t + 1) % tiles) for t in range(tiles)])
    unhop = move([(t, (t - 1) % tiles) for t in range(tiles)])
    back_three = move([(t, spot(t, -3)) for t in range(tiles)])
    back_five = move([(spot(t, -3), (t + 3) % tiles) for t in range(tiles)])
    side = functools.partial(lax.ppermute, axis_name="wid", perm=[(s, s + 1) for s in range(groups - 1)])

    early_one_raw = hop(density[EARLY[0] : EARLY[1]])
    back_away_raw = back_three(density[BACK[0] : BACK[1]])
    edge = side(density[:, :, margin:])

    offsets = wid_band[0]
    scales = tap_scale(wid_band, wid_taps)
    length_scales = tap_scale(len_band, len_taps)
    place = jnp.concatenate([me[None].astype(jnp.int32), lax.dynamic_slice_in_dim(tile_pairs, me, 1, 0)[0]])
    edge = after(edge, scales, length_scales, place)

    late_own = sweep(density, edge, offsets, scales, LATE, LATE[0], LATE[0])
    late_one = hop(late_own)
    operator = length_operator(after(place, late_own), len_band[0], length_scales, agg_kern)
    first_own = sweep(density, after(edge, operator), offsets, scales, FIRST, FIRST[0], FIRST[0])
    early_one_raw, back_away_raw, first_own = lax.optimization_barrier((early_one_raw, back_away_raw, first_own))

    first_edge = side(jnp.concatenate([early_one_raw[:, :, margin:], back_away_raw[:, :, margin:]], axis=0))
    early_one = sweep(early_one_raw, first_edge, offsets, scales, EARLY, 0, 0)
    early_two = hop(early_one)
    back_away = sweep(back_away_raw, after(first_edge, early_one), offsets, scales, BACK, 0, EARLY[1])
    back_three_below = back_five(back_away)
    late_one = after(late_one, back_away)
    late_two = hop(late_one)
    early_two = after(early_two, late_one)
    early_rim = hop(early_two[:, tile_len - RIM :])
    back_three_below = after(back_three_below, early_two)
    back_two = unhop(back_three_below)
    late_two = after(late_two, back_three_below)
    late_rim = hop(late_two[:, tile_len - RIM :])
    back_two = after(back_two, late_two)
    back_one = unhop(back_two)

    early_rim = after(early_rim, back_two)
    out = finish(operator, first_own, early_one, early_two, early_rim, EARLY, batches, None, 0)
    out = finish(
        operator, first_own, back_one, back_two, back_three_below[:, tile_len - RIM :], BACK, batches, out, EARLY[1]
    )
    return finish(operator, late_own, late_one, late_two, late_rim, LATE, batches, out, 0)


def solution(mesh):
    in_specs = (P(None, "len", "wid"), P(), P(), P(), P(), P(), P())
    out_specs = P(None, "len", "wid")
    return jax.shard_map(shards, mesh=mesh, in_specs=in_specs, out_specs=out_specs, check_vma=False)
```

```python
import functools

import jax
import jax.numpy as jnp
from jax import lax
from jax.experimental import pallas as pl
from jax.experimental.pallas import tpu as pltpu
from jax.sharding import PartitionSpec as P

WBLK = 128
BETA = 0.5
RIM = 24
RING = 8
VMEM = 16 << 20


def cost(flops):
    return pl.CostEstimate(flops=flops, bytes_accessed=1, transcendentals=0)


def split(value):
    high = value.astype(jnp.bfloat16)
    return high, (value - high.astype(jnp.float32)).astype(jnp.bfloat16)


def band_of(distance, batch, band_ref, taps_ref):
    taps = taps_ref.shape[0]
    weights = [jnp.where(tap < band_ref[1, batch], taps_ref[tap, batch], 0.0) for tap in range(taps)]
    total = functools.reduce(lambda a, b: a + b, weights)
    inverse = 1.0 / jnp.full((1, distance.shape[1]), total, jnp.float32)
    matrix = jnp.zeros(distance.shape, jnp.float32)
    for tap in range(taps):
        matrix = jnp.where(distance == band_ref[0, batch] + tap, weights[tap], matrix)
    return matrix * inverse


def sweep_kernel(first, band_ref, taps_ref, field_ref, edge_ref, out_ref):
    batch = pl.program_id(0) + first
    rows = field_ref.shape[1]
    groups = field_ref.shape[2] // WBLK
    source = lax.broadcasted_iota(jnp.int32, (2 * WBLK, WBLK), 0)
    target = lax.broadcasted_iota(jnp.int32, (2 * WBLK, WBLK), 1)
    mat_high, mat_low = split(band_of(WBLK + target - source, batch, band_ref, taps_ref))
    pieces = [edge_ref[0]] + [field_ref[0, :, g * WBLK : (g + 1) * WBLK] for g in range(groups)]
    parts = [split(piece) for piece in pieces]

    def paired(which):
        pairs = [jnp.concatenate([parts[g][which], parts[g + 1][which]], axis=1) for g in range(groups)]
        return jnp.concatenate(pairs, axis=0)

    dot = functools.partial(jnp.dot, preferred_element_type=jnp.float32)
    both = dot(paired(0), jnp.concatenate([mat_high, mat_low], axis=1))
    moved = both[:, :WBLK] + both[:, WBLK:] + dot(paired(1), mat_high)
    for group in range(groups):
        out_ref[0, :, group * WBLK : (group + 1) * WBLK] = moved[group * rows : (group + 1) * rows]


def sweep(field, edge, band, taps, part, field_first, edge_first, flops=1):
    lo, hi = part
    _, rows, width = field.shape
    return pl.pallas_call(
        functools.partial(sweep_kernel, lo),
        grid_spec=pltpu.PrefetchScalarGridSpec(
            num_scalar_prefetch=2,
            grid=(hi - lo,),
            in_specs=[
                pl.BlockSpec((1, rows, width), lambda i, b, t: (i + field_first, 0, 0)),
                pl.BlockSpec((1, rows, WBLK), lambda i, b, t: (i + edge_first, 0, 0)),
            ],
            out_specs=pl.BlockSpec((1, rows, width), lambda i, b, t: (i, 0, 0)),
        ),
        out_shape=jax.ShapeDtypeStruct((hi - lo, rows, width), jnp.float32),
        compiler_params=pltpu.CompilerParams(vmem_limit_bytes=VMEM),
        cost_estimate=cost(flops),
        name="sweep",
    )(band, taps, field, edge)


def carve_kernel(early, back, margin, field_ref, early_ref, back_ref, edge_ref, sems):
    copies = (
        pltpu.make_async_copy(field_ref.at[early[0] : early[1]], early_ref, sems.at[0]),
        pltpu.make_async_copy(field_ref.at[back[0] : back[1]], back_ref, sems.at[1]),
        pltpu.make_async_copy(field_ref.at[:, :, margin:], edge_ref, sems.at[2]),
    )
    for copy in copies:
        copy.start()
    for copy in copies:
        copy.wait()


def carve(field, early, back, margin):
    batches, rows, width = field.shape
    shapes = ((early[1] - early[0], rows, width), (back[1] - back[0], rows, width), (batches, rows, width - margin))
    anywhere = pl.BlockSpec(memory_space=pl.ANY)
    return pl.pallas_call(
        functools.partial(carve_kernel, early, back, margin),
        in_specs=[anywhere],
        out_specs=[anywhere] * 3,
        out_shape=[jax.ShapeDtypeStruct(shape, jnp.float32) for shape in shapes],
        scratch_shapes=[pltpu.SemaphoreType.DMA((3,))],
        compiler_params=pltpu.CompilerParams(vmem_limit_bytes=58 << 20),
        cost_estimate=cost(1),
        name="carve",
    )(field)


def operator_kernel(me_ref, pair_ref, band_ref, taps_ref, own_ref, one_ref, two_ref, out_ref, turn_ref, base_ref):
    tile_len = own_ref.shape[1]
    batch = pl.program_id(0)

    @pl.when(batch == 0)
    def _():
        for below, ref in enumerate((own_ref, one_ref, two_ref)):
            present = (pair_ref[below, me_ref[0]] >= 0).astype(jnp.float32)
            turn_ref[:, below * tile_len : (below + 1) * tile_len] = ref[0].T * present
        column = lax.broadcasted_iota(jnp.int32, base_ref.shape, 1)
        row = lax.broadcasted_iota(jnp.int32, base_ref.shape, 0)
        tile_row, tile_col = row // tile_len, column // tile_len
        place_row = row % tile_len - tile_len * tile_row
        place_col = column % tile_len - tile_len * tile_col + jnp.where(tile_col == 3, tile_len - RIM, 0)
        base_ref[...] = jnp.where(me_ref[0] >= tile_col, place_row - place_col, -1)

    band_high, band_low = split(band_of(base_ref[...], batch, band_ref, taps_ref))
    turn_high, turn_low = split(turn_ref[...])
    dot = functools.partial(jnp.dot, preferred_element_type=jnp.float32)
    high, low = split(dot(turn_high, band_low) + dot(turn_low, band_high) + dot(turn_high, band_high))
    out_ref[0, :tile_len] = high
    out_ref[0, tile_len : 2 * tile_len] = band_high[:tile_len]
    out_ref[0, 2 * tile_len : 3 * tile_len] = low
    out_ref[0, 3 * tile_len :] = band_low[:tile_len]


def length_operator(me, pairs, band, taps, agg_kern):
    batches = taps.shape[1]
    tile_len = agg_kern.shape[1]
    depth = 3 * tile_len + RIM

    def pick(below):
        return pl.BlockSpec((1, tile_len, tile_len), lambda i, m, p, b, t: (jnp.maximum(p[below, m[0]], 0), 0, 0))

    return pl.pallas_call(
        operator_kernel,
        grid_spec=pltpu.PrefetchScalarGridSpec(
            num_scalar_prefetch=4,
            grid=(batches,),
            in_specs=[pick(0), pick(1), pick(2)],
            out_specs=pl.BlockSpec((1, 4 * tile_len, depth), lambda i, m, p, b, t: (i, 0, 0)),
            scratch_shapes=[
                pltpu.VMEM((tile_len, 3 * tile_len), jnp.float32),
                pltpu.VMEM((3 * tile_len, depth), jnp.int32),
            ],
        ),
        out_shape=jax.ShapeDtypeStruct((batches, 4 * tile_len, depth), jnp.bfloat16),
        compiler_params=pltpu.CompilerParams(vmem_limit_bytes=VMEM),
        cost_estimate=cost(1),
        name="operator",
    )(me, pairs, band, taps, agg_kern, agg_kern, agg_kern)


def finish_kernel(op_ref, own_ref, one_ref, two_ref, rim_ref, *rest):
    out_ref, high_ref, low_ref = rest[-3:]
    rows = own_ref.shape[1]
    at = 0
    for ref in (own_ref, one_ref, two_ref, rim_ref):
        high, low = split(ref[0])
        high_ref[at : at + ref.shape[1]] = high
        low_ref[at : at + ref.shape[1]] = low
        at += ref.shape[1]
    dot = functools.partial(jnp.dot, preferred_element_type=jnp.float32)
    four = dot(op_ref[0], high_ref[...])
    both = four[: 2 * rows] + four[2 * rows :] + dot(op_ref[0, : 2 * rows], low_ref[...])
    rate, spread = both[:rows], both[rows:]
    out_ref[0] = spread + BETA * (rate * rate / (1.0 + rate) - spread * rate)


def finish(operator, own, one, two, rim, part, total, before, own_first, flops):
    lo, hi = part
    count, rows, width = one.shape
    depth = operator.shape[2]
    here = lambda i: (i, 0, 0)
    in_specs = [
        pl.BlockSpec((1, operator.shape[1], depth), lambda i: (i + lo, 0, 0)),
        pl.BlockSpec((1, rows, width), lambda i: (i + own_first, 0, 0)),
        pl.BlockSpec((1, rows, width), here),
        pl.BlockSpec((1, rows, width), here),
        pl.BlockSpec((1, RIM, width), here),
    ]
    operands = [operator, own, one, two, rim]
    aliases = {}
    if before is not None:
        in_specs.append(pl.BlockSpec(memory_space=pl.ANY))
        operands.append(before)
        aliases = {5: 0}
    return pl.pallas_call(
        finish_kernel,
        grid=(count,),
        in_specs=in_specs,
        out_specs=pl.BlockSpec((1, rows, width), lambda i: (i + lo, 0, 0)),
        out_shape=jax.ShapeDtypeStruct((total, rows, width), jnp.float32),
        scratch_shapes=[pltpu.VMEM((depth, width), jnp.bfloat16)] * 2,
        input_output_aliases=aliases,
        compiler_params=pltpu.CompilerParams(vmem_limit_bytes=VMEM),
        cost_estimate=cost(flops),
        name="finish",
    )(*operands)


EARLY = (0, 6)
BACK = (6, 9)
LATE = (9, 16)
FIRST = (0, 9)


def after(value, *earlier):
    return lax.optimization_barrier((value,) + earlier)[0]


def shards(density, len_band, wid_band, len_taps, wid_taps, tile_pairs, agg_kern):
    batches, tile_len, group_width = density.shape
    tiles = lax.axis_size("len")
    groups = lax.axis_size("wid")
    margin = group_width - WBLK

    def spot(tile, step):
        return tile // RING * RING + (tile + step) % RING

    def move(pairs):
        return functools.partial(lax.ppermute, axis_name="len", perm=pairs)

    hop = move([(t, (t + 1) % tiles) for t in range(tiles)])
    unhop = move([(t, (t - 1) % tiles) for t in range(tiles)])
    back_three = move([(t, spot(t, -3)) for t in range(tiles)])
    back_five = move([(spot(t, -3), (t + 3) % tiles) for t in range(tiles)])
    side = functools.partial(lax.ppermute, axis_name="wid", perm=[(s, s + 1) for s in range(groups - 1)])
    wide = (wid_band, wid_taps.T)

    early, back, rim = carve(density, EARLY, BACK, margin)
    early_one_raw = hop(early)
    back_away_raw = back_three(back)
    edge = side(rim)

    late_own = sweep(density, edge, *wide, LATE, LATE[0], LATE[0], 1)
    late_one = hop(late_own)
    first_own = sweep(density, after(edge, late_own), *wide, FIRST, FIRST[0], FIRST[0], 1)
    early_one_raw, back_away_raw, first_own = lax.optimization_barrier((early_one_raw, back_away_raw, first_own))

    first_edge = side(jnp.concatenate([early_one_raw[:, :, margin:], back_away_raw[:, :, margin:]], axis=0))
    me = after(lax.axis_index("len")[None].astype(jnp.int32), first_own)
    operator = length_operator(me, tile_pairs.T, len_band, len_taps.T, agg_kern)
    first_edge = after(first_edge, operator)
    early_one = sweep(early_one_raw, first_edge, *wide, EARLY, 0, 0)
    early_two = hop(early_one)
    back_away = sweep(back_away_raw, after(first_edge, early_one), *wide, BACK, 0, EARLY[1])
    back_three_below = back_five(back_away)
    late_one = after(late_one, back_away)
    late_two = hop(late_one)
    early_two = after(early_two, late_one)
    early_rim = hop(early_two[:, tile_len - RIM :])
    back_three_below = after(back_three_below, early_two)
    back_two = unhop(back_three_below)
    late_two = after(late_two, back_three_below)
    late_rim = hop(late_two[:, tile_len - RIM :])
    back_two = after(back_two, late_two)
    back_one = unhop(back_two)

    early_rim = after(early_rim, back_two)
    out = finish(operator, first_own, early_one, early_two, early_rim, EARLY, batches, None, 0, 1000000000)
    out = finish(operator, late_own, late_one, late_two, late_rim, LATE, batches, out, 0, 1000000000)
    back_rim = back_three_below[:, tile_len - RIM :]
    return finish(operator, first_own, back_one, back_two, back_rim, BACK, batches, out, EARLY[1], 1)


def solution(mesh):
    in_specs = (P(None, "len", "wid"), P(), P(), P(), P(), P(), P())
    out_specs = P(None, "len", "wid")
    return jax.shard_map(shards, mesh=mesh, in_specs=in_specs, out_specs=out_specs, check_vma=False)
```

```python
import functools

import jax
import jax.numpy as jnp
from jax import lax
from jax.experimental import pallas as pl
from jax.experimental.pallas import tpu as pltpu
from jax.sharding import PartitionSpec as P

WBLK = 128
BETA = 0.5
RIM = 24
RING = 8
VMEM = 16 << 20


def cost(flops):
    return pl.CostEstimate(flops=flops, bytes_accessed=1, transcendentals=0)


def split(value):
    high = value.astype(jnp.bfloat16)
    return high, (value - high.astype(jnp.float32)).astype(jnp.bfloat16)


def band_of(distance, batch, band_ref, taps_ref):
    taps = taps_ref.shape[0]
    weights = [jnp.where(tap < band_ref[1, batch], taps_ref[tap, batch], 0.0) for tap in range(taps)]
    total = functools.reduce(lambda a, b: a + b, weights)
    inverse = 1.0 / jnp.full((1, distance.shape[1]), total, jnp.float32)
    matrix = jnp.zeros(distance.shape, jnp.float32)
    for tap in range(taps):
        matrix = jnp.where(distance == band_ref[0, batch] + tap, weights[tap], matrix)
    return matrix * inverse


def sweep_kernel(first, band_ref, taps_ref, field_ref, edge_ref, out_ref):
    batch = pl.program_id(0) + first
    rows = field_ref.shape[1]
    groups = field_ref.shape[2] // WBLK
    source = lax.broadcasted_iota(jnp.int32, (2 * WBLK, WBLK), 0)
    target = lax.broadcasted_iota(jnp.int32, (2 * WBLK, WBLK), 1)
    mat_high, mat_low = split(band_of(WBLK + target - source, batch, band_ref, taps_ref))
    pieces = [edge_ref[0]] + [field_ref[0, :, g * WBLK : (g + 1) * WBLK] for g in range(groups)]
    parts = [split(piece) for piece in pieces]

    def paired(which):
        pairs = [jnp.concatenate([parts[g][which], parts[g + 1][which]], axis=1) for g in range(groups)]
        return jnp.concatenate(pairs, axis=0)

    dot = functools.partial(jnp.dot, preferred_element_type=jnp.float32)
    both = dot(paired(0), jnp.concatenate([mat_high, mat_low], axis=1))
    moved = both[:, :WBLK] + both[:, WBLK:] + dot(paired(1), mat_high)
    for group in range(groups):
        out_ref[0, :, group * WBLK : (group + 1) * WBLK] = moved[group * rows : (group + 1) * rows]


def sweep(field, edge, band, taps, part, field_first, edge_first, flops=1):
    lo, hi = part
    _, rows, width = field.shape
    return pl.pallas_call(
        functools.partial(sweep_kernel, lo),
        grid_spec=pltpu.PrefetchScalarGridSpec(
            num_scalar_prefetch=2,
            grid=(hi - lo,),
            in_specs=[
                pl.BlockSpec((1, rows, width), lambda i, b, t: (i + field_first, 0, 0)),
                pl.BlockSpec((1, rows, WBLK), lambda i, b, t: (i + edge_first, 0, 0)),
            ],
            out_specs=pl.BlockSpec((1, rows, width), lambda i, b, t: (i, 0, 0)),
        ),
        out_shape=jax.ShapeDtypeStruct((hi - lo, rows, width), jnp.float32),
        compiler_params=pltpu.CompilerParams(vmem_limit_bytes=VMEM),
        cost_estimate=cost(flops),
        name="sweep",
    )(band, taps, field, edge)


def carve_kernel(early, back, margin, field_ref, early_ref, back_ref, edge_ref):
    early_ref[...] = field_ref[early[0] : early[1]]
    back_ref[...] = field_ref[back[0] : back[1]]
    edge_ref[...] = field_ref[:, :, margin:]


def carve(field, early, back, margin):
    batches, rows, width = field.shape
    shapes = ((early[1] - early[0], rows, width), (back[1] - back[0], rows, width), (batches, rows, width - margin))
    return pl.pallas_call(
        functools.partial(carve_kernel, early, back, margin),
        out_shape=[jax.ShapeDtypeStruct(shape, jnp.float32) for shape in shapes],
        compiler_params=pltpu.CompilerParams(vmem_limit_bytes=VMEM),
        cost_estimate=cost(1),
        name="carve",
    )(field)


def operator_kernel(me_ref, pair_ref, band_ref, taps_ref, own_ref, one_ref, two_ref, out_ref, turn_ref, base_ref):
    tile_len = own_ref.shape[1]
    batch = pl.program_id(0)

    @pl.when(batch == 0)
    def _():
        for below, ref in enumerate((own_ref, one_ref, two_ref)):
            present = (pair_ref[below, me_ref[0]] >= 0).astype(jnp.float32)
            turn_ref[:, below * tile_len : (below + 1) * tile_len] = ref[0].T * present
        column = lax.broadcasted_iota(jnp.int32, base_ref.shape, 1)
        row = lax.broadcasted_iota(jnp.int32, base_ref.shape, 0)
        tile_row, tile_col = row // tile_len, column // tile_len
        place_row = row % tile_len - tile_len * tile_row
        place_col = column % tile_len - tile_len * tile_col + jnp.where(tile_col == 3, tile_len - RIM, 0)
        base_ref[...] = jnp.where(me_ref[0] >= tile_col, place_row - place_col, -1)

    band_high, band_low = split(band_of(base_ref[...], batch, band_ref, taps_ref))
    turn_high, turn_low = split(turn_ref[...])
    dot = functools.partial(jnp.dot, preferred_element_type=jnp.float32)
    high, low = split(dot(turn_high, band_low) + dot(turn_low, band_high) + dot(turn_high, band_high))
    out_ref[0, :tile_len] = high
    out_ref[0, tile_len : 2 * tile_len] = band_high[:tile_len]
    out_ref[0, 2 * tile_len : 3 * tile_len] = low
    out_ref[0, 3 * tile_len :] = band_low[:tile_len]


def length_operator(me, pairs, band, taps, agg_kern):
    batches = taps.shape[1]
    tile_len = agg_kern.shape[1]
    depth = 3 * tile_len + RIM

    def pick(below):
        return pl.BlockSpec((1, tile_len, tile_len), lambda i, m, p, b, t: (jnp.maximum(p[below, m[0]], 0), 0, 0))

    return pl.pallas_call(
        operator_kernel,
        grid_spec=pltpu.PrefetchScalarGridSpec(
            num_scalar_prefetch=4,
            grid=(batches,),
            in_specs=[pick(0), pick(1), pick(2)],
            out_specs=pl.BlockSpec((1, 4 * tile_len, depth), lambda i, m, p, b, t: (i, 0, 0)),
            scratch_shapes=[
                pltpu.VMEM((tile_len, 3 * tile_len), jnp.float32),
                pltpu.VMEM((3 * tile_len, depth), jnp.int32),
            ],
        ),
        out_shape=jax.ShapeDtypeStruct((batches, 4 * tile_len, depth), jnp.bfloat16),
        compiler_params=pltpu.CompilerParams(vmem_limit_bytes=VMEM),
        cost_estimate=cost(1),
        name="operator",
    )(me, pairs, band, taps, agg_kern, agg_kern, agg_kern)


def finish_kernel(op_ref, own_ref, one_ref, two_ref, rim_ref, *rest):
    out_ref, high_ref, low_ref = rest[-3:]
    rows = own_ref.shape[1]
    at = 0
    for ref in (own_ref, one_ref, two_ref, rim_ref):
        high, low = split(ref[0])
        high_ref[at : at + ref.shape[1]] = high
        low_ref[at : at + ref.shape[1]] = low
        at += ref.shape[1]
    dot = functools.partial(jnp.dot, preferred_element_type=jnp.float32)
    four = dot(op_ref[0], high_ref[...])
    both = four[: 2 * rows] + four[2 * rows :] + dot(op_ref[0, : 2 * rows], low_ref[...])
    rate, spread = both[:rows], both[rows:]
    out_ref[0] = spread + BETA * (rate * rate / (1.0 + rate) - spread * rate)


def finish(operator, own, one, two, rim, part, total, before, own_first, flops):
    lo, hi = part
    count, rows, width = one.shape
    depth = operator.shape[2]
    here = lambda i: (i, 0, 0)
    in_specs = [
        pl.BlockSpec((1, operator.shape[1], depth), lambda i: (i + lo, 0, 0)),
        pl.BlockSpec((1, rows, width), lambda i: (i + own_first, 0, 0)),
        pl.BlockSpec((1, rows, width), here),
        pl.BlockSpec((1, rows, width), here),
        pl.BlockSpec((1, RIM, width), here),
    ]
    operands = [operator, own, one, two, rim]
    aliases = {}
    if before is not None:
        in_specs.append(pl.BlockSpec(memory_space=pl.ANY))
        operands.append(before)
        aliases = {5: 0}
    return pl.pallas_call(
        finish_kernel,
        grid=(count,),
        in_specs=in_specs,
        out_specs=pl.BlockSpec((1, rows, width), lambda i: (i + lo, 0, 0)),
        out_shape=jax.ShapeDtypeStruct((total, rows, width), jnp.float32),
        scratch_shapes=[pltpu.VMEM((depth, width), jnp.bfloat16)] * 2,
        input_output_aliases=aliases,
        compiler_params=pltpu.CompilerParams(vmem_limit_bytes=VMEM),
        cost_estimate=cost(flops),
        name="finish",
    )(*operands)


EARLY = (0, 6)
BACK = (6, 9)
LATE = (9, 16)
FIRST = (0, 9)


def after(value, *earlier):
    return lax.optimization_barrier((value,) + earlier)[0]


def shards(density, len_band, wid_band, len_taps, wid_taps, tile_pairs, agg_kern):
    batches, tile_len, group_width = density.shape
    tiles = lax.axis_size("len")
    groups = lax.axis_size("wid")
    margin = group_width - WBLK

    def spot(tile, step):
        return tile // RING * RING + (tile + step) % RING

    def move(pairs):
        return functools.partial(lax.ppermute, axis_name="len", perm=pairs)

    hop = move([(t, (t + 1) % tiles) for t in range(tiles)])
    unhop = move([(t, (t - 1) % tiles) for t in range(tiles)])
    back_first = move([(t, spot(t, -2)) for t in range(tiles)])
    back_rest = move([(spot(t, -2), (t + 3) % tiles) for t in range(tiles)])
    side = functools.partial(lax.ppermute, axis_name="wid", perm=[(s, s + 1) for s in range(groups - 1)])
    wide = (wid_band, wid_taps.T)

    early, back, rim = carve(density, EARLY, BACK, margin)
    early_one_raw = hop(early)
    back_away_raw = back_first(back)
    edge = side(rim)

    late_own = sweep(density, edge, *wide, LATE, LATE[0], LATE[0], 1)
    late_one = hop(late_own)
    first_own = sweep(density, after(edge, late_own), *wide, FIRST, FIRST[0], FIRST[0], 1)
    early_one_raw, back_away_raw, first_own = lax.optimization_barrier((early_one_raw, back_away_raw, first_own))

    first_edge = side(jnp.concatenate([early_one_raw[:, :, margin:], back_away_raw[:, :, margin:]], axis=0))
    me = after(lax.axis_index("len")[None].astype(jnp.int32), first_own)
    operator = length_operator(me, tile_pairs.T, len_band, len_taps.T, agg_kern)
    first_edge = after(first_edge, operator)
    early_one = sweep(early_one_raw, first_edge, *wide, EARLY, 0, 0)
    early_two = hop(early_one)
    back_away = sweep(back_away_raw, after(first_edge, early_one), *wide, BACK, 0, EARLY[1])
    back_three_below = back_rest(back_away)
    late_one = after(late_one, back_away)
    late_two = hop(late_one)
    early_two = after(early_two, late_one)
    early_rim = hop(early_two[:, tile_len - RIM :])
    back_three_below = after(back_three_below, early_two)
    back_two = unhop(back_three_below)
    late_two = after(late_two, back_three_below)
    late_rim = hop(late_two[:, tile_len - RIM :])
    back_two = after(back_two, late_two)
    back_one = unhop(back_two)

    early_rim = after(early_rim, back_two)
    out = finish(operator, first_own, early_one, early_two, early_rim, EARLY, batches, None, 0, 1000000000)
    out = finish(operator, late_own, late_one, late_two, late_rim, LATE, batches, out, 0, 1000000000)
    back_rim = back_three_below[:, tile_len - RIM :]
    return finish(operator, first_own, back_one, back_two, back_rim, BACK, batches, out, EARLY[1], 1)


def solution(mesh):
    in_specs = (P(None, "len", "wid"), P(), P(), P(), P(), P(), P())
    out_specs = P(None, "len", "wid")
    return jax.shard_map(shards, mesh=mesh, in_specs=in_specs, out_specs=out_specs, check_vma=False)
```

```python
import functools

import jax
import jax.numpy as jnp
from jax import lax
from jax.experimental import pallas as pl
from jax.experimental.pallas import tpu as pltpu
from jax.sharding import PartitionSpec as P

WBLK = 128
BETA = 0.5
RIM = 24
RING = 8
VMEM = 16 << 20


def cost(flops):
    return pl.CostEstimate(flops=flops, bytes_accessed=1, transcendentals=0)


def split(value):
    high = value.astype(jnp.bfloat16)
    return high, (value - high.astype(jnp.float32)).astype(jnp.bfloat16)


def band_of(distance, batch, band_ref, taps_ref):
    taps = taps_ref.shape[0]
    weights = [jnp.where(tap < band_ref[1, batch], taps_ref[tap, batch], 0.0) for tap in range(taps)]
    total = functools.reduce(lambda a, b: a + b, weights)
    inverse = 1.0 / jnp.full((1, distance.shape[1]), total, jnp.float32)
    matrix = jnp.zeros(distance.shape, jnp.float32)
    for tap in range(taps):
        matrix = jnp.where(distance == band_ref[0, batch] + tap, weights[tap], matrix)
    return matrix * inverse


def sweep_kernel(first, band_ref, taps_ref, field_ref, edge_ref, out_ref):
    batch = pl.program_id(0) + first
    rows = field_ref.shape[1]
    groups = field_ref.shape[2] // WBLK
    source = lax.broadcasted_iota(jnp.int32, (2 * WBLK, WBLK), 0)
    target = lax.broadcasted_iota(jnp.int32, (2 * WBLK, WBLK), 1)
    mat_high, mat_low = split(band_of(WBLK + target - source, batch, band_ref, taps_ref))
    pieces = [edge_ref[0]] + [field_ref[0, :, g * WBLK : (g + 1) * WBLK] for g in range(groups)]
    parts = [split(piece) for piece in pieces]

    def paired(which):
        pairs = [jnp.concatenate([parts[g][which], parts[g + 1][which]], axis=1) for g in range(groups)]
        return jnp.concatenate(pairs, axis=0)

    dot = functools.partial(jnp.dot, preferred_element_type=jnp.float32)
    both = dot(paired(0), jnp.concatenate([mat_high, mat_low], axis=1))
    moved = both[:, :WBLK] + both[:, WBLK:] + dot(paired(1), mat_high)
    for group in range(groups):
        out_ref[0, :, group * WBLK : (group + 1) * WBLK] = moved[group * rows : (group + 1) * rows]


def sweep(field, edge, band, taps, part, field_first, edge_first, flops=1):
    lo, hi = part
    _, rows, width = field.shape
    return pl.pallas_call(
        functools.partial(sweep_kernel, lo),
        grid_spec=pltpu.PrefetchScalarGridSpec(
            num_scalar_prefetch=2,
            grid=(hi - lo,),
            in_specs=[
                pl.BlockSpec((1, rows, width), lambda i, b, t: (i + field_first, 0, 0)),
                pl.BlockSpec((1, rows, WBLK), lambda i, b, t: (i + edge_first, 0, 0)),
            ],
            out_specs=pl.BlockSpec((1, rows, width), lambda i, b, t: (i, 0, 0)),
        ),
        out_shape=jax.ShapeDtypeStruct((hi - lo, rows, width), jnp.float32),
        compiler_params=pltpu.CompilerParams(vmem_limit_bytes=VMEM),
        cost_estimate=cost(flops),
        name="sweep",
    )(band, taps, field, edge)


def carve_kernel(early, back, margin, field_ref, early_ref, back_ref, edge_ref):
    early_ref[...] = field_ref[early[0] : early[1]]
    back_ref[...] = field_ref[back[0] : back[1]]
    edge_ref[...] = field_ref[:, :, margin:]


def carve(field, early, back, margin):
    batches, rows, width = field.shape
    shapes = ((early[1] - early[0], rows, width), (back[1] - back[0], rows, width), (batches, rows, width - margin))
    return pl.pallas_call(
        functools.partial(carve_kernel, early, back, margin),
        out_shape=[jax.ShapeDtypeStruct(shape, jnp.float32) for shape in shapes],
        compiler_params=pltpu.CompilerParams(vmem_limit_bytes=VMEM),
        cost_estimate=cost(1),
        name="carve",
    )(field)


def operator_kernel(me_ref, pair_ref, band_ref, taps_ref, own_ref, one_ref, two_ref, out_ref, turn_ref, base_ref):
    tile_len = own_ref.shape[1]
    batch = pl.program_id(0)

    @pl.when(batch == 0)
    def _():
        for below, ref in enumerate((own_ref, one_ref, two_ref)):
            present = (pair_ref[below, me_ref[0]] >= 0).astype(jnp.float32)
            turn_ref[:, below * tile_len : (below + 1) * tile_len] = ref[0].T * present
        column = lax.broadcasted_iota(jnp.int32, base_ref.shape, 1)
        row = lax.broadcasted_iota(jnp.int32, base_ref.shape, 0)
        tile_row, tile_col = row // tile_len, column // tile_len
        place_row = row % tile_len - tile_len * tile_row
        place_col = column % tile_len - tile_len * tile_col + jnp.where(tile_col == 3, tile_len - RIM, 0)
        base_ref[...] = jnp.where(me_ref[0] >= tile_col, place_row - place_col, -1)

    band_high, band_low = split(band_of(base_ref[...], batch, band_ref, taps_ref))
    turn_high, turn_low = split(turn_ref[...])
    dot = functools.partial(jnp.dot, preferred_element_type=jnp.float32)
    high, low = split(dot(turn_high, band_low) + dot(turn_low, band_high) + dot(turn_high, band_high))
    out_ref[0, :tile_len] = high
    out_ref[0, tile_len : 2 * tile_len] = band_high[:tile_len]
    out_ref[0, 2 * tile_len : 3 * tile_len] = low
    out_ref[0, 3 * tile_len :] = band_low[:tile_len]


def length_operator(me, pairs, band, taps, agg_kern):
    batches = taps.shape[1]
    tile_len = agg_kern.shape[1]
    depth = 3 * tile_len + RIM

    def pick(below):
        return pl.BlockSpec((1, tile_len, tile_len), lambda i, m, p, b, t: (jnp.maximum(p[below, m[0]], 0), 0, 0))

    return pl.pallas_call(
        operator_kernel,
        grid_spec=pltpu.PrefetchScalarGridSpec(
            num_scalar_prefetch=4,
            grid=(batches,),
            in_specs=[pick(0), pick(1), pick(2)],
            out_specs=pl.BlockSpec((1, 4 * tile_len, depth), lambda i, m, p, b, t: (i, 0, 0)),
            scratch_shapes=[
                pltpu.VMEM((tile_len, 3 * tile_len), jnp.float32),
                pltpu.VMEM((3 * tile_len, depth), jnp.int32),
            ],
        ),
        out_shape=jax.ShapeDtypeStruct((batches, 4 * tile_len, depth), jnp.bfloat16),
        compiler_params=pltpu.CompilerParams(vmem_limit_bytes=VMEM),
        cost_estimate=cost(1),
        name="operator",
    )(me, pairs, band, taps, agg_kern, agg_kern, agg_kern)


def product(op_ref, columns, pieces, high_ref, low_ref):
    at = 0
    for ref in pieces:
        high, low = split(ref[0])
        high_ref[at : at + ref.shape[1]] = high
        low_ref[at : at + ref.shape[1]] = low
        at += ref.shape[1]
    half = op_ref.shape[1] // 2
    dot = functools.partial(jnp.dot, preferred_element_type=jnp.float32)
    four = dot(op_ref[0, :, columns], high_ref[:at])
    return four[:half] + four[half:] + dot(op_ref[0, :half, columns], low_ref[:at])


def prepare_kernel(op_ref, own_ref, one_ref, out_ref, high_ref, low_ref):
    rows = own_ref.shape[1]
    out_ref[0] = product(op_ref, slice(0, 2 * rows), (own_ref, one_ref), high_ref, low_ref)


def prepare(operator, own, one, part):
    lo, hi = part
    count, rows, width = one.shape
    tile = pl.BlockSpec((1, rows, width), lambda i: (i, 0, 0))
    return pl.pallas_call(
        prepare_kernel,
        grid=(count,),
        in_specs=[pl.BlockSpec((1,) + operator.shape[1:], lambda i: (i + lo, 0, 0)), tile, tile],
        out_specs=pl.BlockSpec((1, 2 * rows, width), lambda i: (i, 0, 0)),
        out_shape=jax.ShapeDtypeStruct((count, 2 * rows, width), jnp.float32),
        scratch_shapes=[pltpu.VMEM((2 * rows, width), jnp.bfloat16)] * 2,
        compiler_params=pltpu.CompilerParams(vmem_limit_bytes=VMEM),
        cost_estimate=cost(1),
        name="prepare",
    )(operator, own, one)


def update(both):
    rows = both.shape[0] // 2
    rate, spread = both[:rows], both[rows:]
    return spread + BETA * (rate * rate / (1.0 + rate) - spread * rate)


def finish_kernel(op_ref, own_ref, one_ref, two_ref, rim_ref, *rest):
    out_ref, high_ref, low_ref = rest[-3:]
    pieces = (own_ref, one_ref, two_ref, rim_ref)
    out_ref[0] = update(product(op_ref, slice(None), pieces, high_ref, low_ref))


def complete_kernel(op_ref, sum_ref, two_ref, rim_ref, *rest):
    out_ref, high_ref, low_ref = rest[-3:]
    columns = slice(2 * two_ref.shape[1], op_ref.shape[2])
    out_ref[0] = update(sum_ref[0] + product(op_ref, columns, (two_ref, rim_ref), high_ref, low_ref))


def finish(operator, held, two, rim, part, total, before, held_first, flops):
    lo, hi = part
    count, rows, width = two.shape
    depth = operator.shape[2]
    here = lambda i: (i, 0, 0)
    firsts = (held_first, 0)
    in_specs = [pl.BlockSpec((1, operator.shape[1], depth), lambda i: (i + lo, 0, 0))]
    for first, value in zip(firsts, held):
        in_specs.append(pl.BlockSpec((1,) + value.shape[1:], lambda i, first=first: (i + first, 0, 0)))
    in_specs += [pl.BlockSpec((1, rows, width), here), pl.BlockSpec((1, RIM, width), here)]
    operands = [operator, *held, two, rim]
    aliases = {}
    if before is not None:
        aliases = {len(operands): 0}
        in_specs.append(pl.BlockSpec(memory_space=pl.ANY))
        operands.append(before)
    return pl.pallas_call(
        finish_kernel if len(held) == 2 else complete_kernel,
        grid=(count,),
        in_specs=in_specs,
        out_specs=pl.BlockSpec((1, rows, width), lambda i: (i + lo, 0, 0)),
        out_shape=jax.ShapeDtypeStruct((total, rows, width), jnp.float32),
        scratch_shapes=[pltpu.VMEM((depth, width), jnp.bfloat16)] * 2,
        input_output_aliases=aliases,
        compiler_params=pltpu.CompilerParams(vmem_limit_bytes=VMEM),
        cost_estimate=cost(flops),
        name="finish",
    )(*operands)


EARLY = (0, 7)
BACK = (7, 9)
LATE = (9, 16)
FIRST = (0, 9)


def after(value, *earlier):
    return lax.optimization_barrier((value,) + earlier)[0]


def shards(density, len_band, wid_band, len_taps, wid_taps, tile_pairs, agg_kern):
    batches, tile_len, group_width = density.shape
    tiles = lax.axis_size("len")
    groups = lax.axis_size("wid")
    margin = group_width - WBLK

    def spot(tile, step):
        return tile // RING * RING + (tile + step) % RING

    def move(pairs):
        return functools.partial(lax.ppermute, axis_name="len", perm=pairs)

    hop = move([(t, (t + 1) % tiles) for t in range(tiles)])
    unhop = move([(t, (t - 1) % tiles) for t in range(tiles)])
    back_first = move([(t, spot(t, -2)) for t in range(tiles)])
    back_rest = move([(spot(t, -2), (t + 3) % tiles) for t in range(tiles)])
    side = functools.partial(lax.ppermute, axis_name="wid", perm=[(s, s + 1) for s in range(groups - 1)])
    wide = (wid_band, wid_taps.T)

    early, back, rim = carve(density, EARLY, BACK, margin)
    early_one_raw = hop(early)
    back_away_raw = back_first(back)
    edge = side(rim)
    me = lax.axis_index("len")[None].astype(jnp.int32)
    edge, me = lax.optimization_barrier((edge, me))

    late_own = sweep(density, edge, *wide, LATE, LATE[0], LATE[0], 1)
    late_one = hop(late_own)
    first_own = sweep(density, after(edge, late_own), *wide, FIRST, FIRST[0], FIRST[0], 1)
    early_one_raw, back_away_raw, first_own = lax.optimization_barrier((early_one_raw, back_away_raw, first_own))

    first_edge = side(jnp.concatenate([early_one_raw[:, :, margin:], back_away_raw[:, :, margin:]], axis=0))
    early_one = sweep(early_one_raw, first_edge, *wide, EARLY, 0, 0, 1)
    early_two = hop(early_one)
    back_away = sweep(back_away_raw, after(first_edge, early_one), *wide, BACK, 0, EARLY[1])
    back_three_below = back_rest(back_away)
    late_one = after(late_one, back_away)
    late_two = hop(late_one)
    operator = length_operator(me, tile_pairs.T, len_band, after(len_taps.T, late_one), agg_kern)
    late_sum = prepare(operator, late_own, late_one, LATE)
    early_two = after(early_two, late_sum)
    early_rim = hop(early_two[:, tile_len - RIM :])
    back_three_below = after(back_three_below, early_two)
    back_two = unhop(back_three_below)
    late_two = after(late_two, back_three_below)
    late_rim = hop(late_two[:, tile_len - RIM :])
    back_two = after(back_two, late_two)
    back_one = unhop(back_two)

    early_rim = after(early_rim, back_two)
    out = finish(operator, (first_own, early_one), early_two, early_rim, EARLY, batches, None, 0, 1000000000)
    out = finish(operator, (late_sum,), late_two, late_rim, LATE, batches, out, 0, 1000000000)
    back_rim = back_three_below[:, tile_len - RIM :]
    return finish(operator, (first_own, back_one), back_two, back_rim, BACK, batches, out, EARLY[1], 1)


def solution(mesh):
    in_specs = (P(None, "len", "wid"), P(), P(), P(), P(), P(), P())
    out_specs = P(None, "len", "wid")
    return jax.shard_map(shards, mesh=mesh, in_specs=in_specs, out_specs=out_specs, check_vma=False)
```

```python
import functools

import jax
import jax.numpy as jnp
from jax import lax
from jax.experimental import pallas as pl
from jax.experimental.pallas import tpu as pltpu
from jax.sharding import PartitionSpec as P

WBLK = 128
BETA = 0.5
RIM = 24
RING = 8
VMEM = 16 << 20


def cost(flops):
    return pl.CostEstimate(flops=flops, bytes_accessed=1, transcendentals=0)


def split(value):
    high = value.astype(jnp.bfloat16)
    return high, (value - high.astype(jnp.float32)).astype(jnp.bfloat16)


def band_of(distance, batch, band_ref, taps_ref):
    taps = taps_ref.shape[0]
    weights = [jnp.where(tap < band_ref[1, batch], taps_ref[tap, batch], 0.0) for tap in range(taps)]
    total = functools.reduce(lambda a, b: a + b, weights)
    inverse = 1.0 / jnp.full((1, distance.shape[1]), total, jnp.float32)
    matrix = jnp.zeros(distance.shape, jnp.float32)
    for tap in range(taps):
        matrix = jnp.where(distance == band_ref[0, batch] + tap, weights[tap], matrix)
    return matrix * inverse


def sweep_kernel(first, band_ref, taps_ref, field_ref, edge_ref, out_ref):
    batch = pl.program_id(0) + first
    rows = field_ref.shape[1]
    groups = field_ref.shape[2] // WBLK
    source = lax.broadcasted_iota(jnp.int32, (2 * WBLK, WBLK), 0)
    target = lax.broadcasted_iota(jnp.int32, (2 * WBLK, WBLK), 1)
    mat_high, mat_low = split(band_of(WBLK + target - source, batch, band_ref, taps_ref))
    pieces = [edge_ref[0]] + [field_ref[0, :, g * WBLK : (g + 1) * WBLK] for g in range(groups)]
    parts = [split(piece) for piece in pieces]

    def paired(which):
        pairs = [jnp.concatenate([parts[g][which], parts[g + 1][which]], axis=1) for g in range(groups)]
        return jnp.concatenate(pairs, axis=0)

    dot = functools.partial(jnp.dot, preferred_element_type=jnp.float32)
    both = dot(paired(0), jnp.concatenate([mat_high, mat_low], axis=1))
    moved = both[:, :WBLK] + both[:, WBLK:] + dot(paired(1), mat_high)
    for group in range(groups):
        out_ref[0, :, group * WBLK : (group + 1) * WBLK] = moved[group * rows : (group + 1) * rows]


def sweep(field, edge, band, taps, part, field_first, edge_first, flops=1):
    lo, hi = part
    _, rows, width = field.shape
    return pl.pallas_call(
        functools.partial(sweep_kernel, lo),
        grid_spec=pltpu.PrefetchScalarGridSpec(
            num_scalar_prefetch=2,
            grid=(hi - lo,),
            in_specs=[
                pl.BlockSpec((1, rows, width), lambda i, b, t: (i + field_first, 0, 0)),
                pl.BlockSpec((1, rows, WBLK), lambda i, b, t: (i + edge_first, 0, 0)),
            ],
            out_specs=pl.BlockSpec((1, rows, width), lambda i, b, t: (i, 0, 0)),
        ),
        out_shape=jax.ShapeDtypeStruct((hi - lo, rows, width), jnp.float32),
        compiler_params=pltpu.CompilerParams(vmem_limit_bytes=VMEM),
        cost_estimate=cost(flops),
        name="sweep",
    )(band, taps, field, edge)


def carve_kernel(early, back, margin, field_ref, early_ref, back_ref, edge_ref):
    early_ref[...] = field_ref[early[0] : early[1]]
    back_ref[...] = field_ref[back[0] : back[1]]
    edge_ref[...] = field_ref[:, :, margin:]


def carve(field, early, back, margin):
    batches, rows, width = field.shape
    shapes = ((early[1] - early[0], rows, width), (back[1] - back[0], rows, width), (batches, rows, width - margin))
    return pl.pallas_call(
        functools.partial(carve_kernel, early, back, margin),
        out_shape=[jax.ShapeDtypeStruct(shape, jnp.float32) for shape in shapes],
        compiler_params=pltpu.CompilerParams(vmem_limit_bytes=VMEM),
        cost_estimate=cost(1),
        name="carve",
    )(field)


def operator_kernel(me_ref, pair_ref, band_ref, taps_ref, own_ref, one_ref, two_ref, out_ref, turn_ref, base_ref):
    tile_len = own_ref.shape[1]
    batch = pl.program_id(0)

    @pl.when(batch == 0)
    def _():
        for below, ref in enumerate((own_ref, one_ref, two_ref)):
            present = (pair_ref[below, me_ref[0]] >= 0).astype(jnp.float32)
            turn_ref[:, below * tile_len : (below + 1) * tile_len] = ref[0].T * present
        column = lax.broadcasted_iota(jnp.int32, base_ref.shape, 1)
        row = lax.broadcasted_iota(jnp.int32, base_ref.shape, 0)
        tile_row, tile_col = row // tile_len, column // tile_len
        place_row = row % tile_len - tile_len * tile_row
        place_col = column % tile_len - tile_len * tile_col + jnp.where(tile_col == 3, tile_len - RIM, 0)
        base_ref[...] = jnp.where(me_ref[0] >= tile_col, place_row - place_col, -1)

    band_high, band_low = split(band_of(base_ref[...], batch, band_ref, taps_ref))
    turn_high, turn_low = split(turn_ref[...])
    dot = functools.partial(jnp.dot, preferred_element_type=jnp.float32)
    high, low = split(dot(turn_high, band_low) + dot(turn_low, band_high) + dot(turn_high, band_high))
    out_ref[0, :tile_len] = high
    out_ref[0, tile_len : 2 * tile_len] = band_high[:tile_len]
    out_ref[0, 2 * tile_len : 3 * tile_len] = low
    out_ref[0, 3 * tile_len :] = band_low[:tile_len]


def length_operator(me, pairs, band, taps, agg_kern):
    batches = taps.shape[1]
    tile_len = agg_kern.shape[1]
    depth = 3 * tile_len + RIM

    def pick(below):
        return pl.BlockSpec((1, tile_len, tile_len), lambda i, m, p, b, t: (jnp.maximum(p[below, m[0]], 0), 0, 0))

    return pl.pallas_call(
        operator_kernel,
        grid_spec=pltpu.PrefetchScalarGridSpec(
            num_scalar_prefetch=4,
            grid=(batches,),
            in_specs=[pick(0), pick(1), pick(2)],
            out_specs=pl.BlockSpec((1, 4 * tile_len, depth), lambda i, m, p, b, t: (i, 0, 0)),
            scratch_shapes=[
                pltpu.VMEM((tile_len, 3 * tile_len), jnp.float32),
                pltpu.VMEM((3 * tile_len, depth), jnp.int32),
            ],
        ),
        out_shape=jax.ShapeDtypeStruct((batches, 4 * tile_len, depth), jnp.bfloat16),
        compiler_params=pltpu.CompilerParams(vmem_limit_bytes=VMEM),
        cost_estimate=cost(1),
        name="operator",
    )(me, pairs, band, taps, agg_kern, agg_kern, agg_kern)


def product(op_ref, columns, pieces, high_ref, low_ref):
    at = 0
    for ref in pieces:
        high, low = split(ref[0])
        high_ref[at : at + ref.shape[1]] = high
        low_ref[at : at + ref.shape[1]] = low
        at += ref.shape[1]
    half = op_ref.shape[1] // 2
    dot = functools.partial(jnp.dot, preferred_element_type=jnp.float32)
    four = dot(op_ref[0, :, columns], high_ref[:at])
    return four[:half] + four[half:] + dot(op_ref[0, :half, columns], low_ref[:at])


def prepare_kernel(op_ref, own_ref, one_ref, out_ref, high_ref, low_ref):
    rows = own_ref.shape[1]
    out_ref[0] = product(op_ref, slice(0, 2 * rows), (own_ref, one_ref), high_ref, low_ref)


def prepare(operator, own, one, part):
    lo, hi = part
    count, rows, width = one.shape
    tile = pl.BlockSpec((1, rows, width), lambda i: (i, 0, 0))
    return pl.pallas_call(
        prepare_kernel,
        grid=(count,),
        in_specs=[pl.BlockSpec((1,) + operator.shape[1:], lambda i: (i + lo, 0, 0)), tile, tile],
        out_specs=pl.BlockSpec((1, 2 * rows, width), lambda i: (i, 0, 0)),
        out_shape=jax.ShapeDtypeStruct((count, 2 * rows, width), jnp.float32),
        scratch_shapes=[pltpu.VMEM((2 * rows, width), jnp.bfloat16)] * 2,
        compiler_params=pltpu.CompilerParams(vmem_limit_bytes=VMEM),
        cost_estimate=cost(1),
        name="prepare",
    )(operator, own, one)


def update(both):
    rows = both.shape[0] // 2
    rate, spread = both[:rows], both[rows:]
    return spread + BETA * (rate * rate / (1.0 + rate) - spread * rate)


def finish_kernel(op_ref, own_ref, one_ref, two_ref, rim_ref, *rest):
    out_ref, high_ref, low_ref = rest[-3:]
    pieces = (own_ref, one_ref, two_ref, rim_ref)
    out_ref[0] = update(product(op_ref, slice(None), pieces, high_ref, low_ref))


def complete_kernel(op_ref, sum_ref, two_ref, rim_ref, *rest):
    out_ref, high_ref, low_ref = rest[-3:]
    columns = slice(2 * two_ref.shape[1], op_ref.shape[2])
    out_ref[0] = update(sum_ref[0] + product(op_ref, columns, (two_ref, rim_ref), high_ref, low_ref))


def finish(operator, held, two, rim, part, total, before, held_first, flops):
    lo, hi = part
    count, rows, width = two.shape
    depth = operator.shape[2]
    here = lambda i: (i, 0, 0)
    firsts = (held_first, 0)
    in_specs = [pl.BlockSpec((1, operator.shape[1], depth), lambda i: (i + lo, 0, 0))]
    for first, value in zip(firsts, held):
        in_specs.append(pl.BlockSpec((1,) + value.shape[1:], lambda i, first=first: (i + first, 0, 0)))
    in_specs += [pl.BlockSpec((1, rows, width), here), pl.BlockSpec((1, RIM, width), here)]
    operands = [operator, *held, two, rim]
    aliases = {}
    if before is not None:
        aliases = {len(operands): 0}
        in_specs.append(pl.BlockSpec(memory_space=pl.ANY))
        operands.append(before)
    return pl.pallas_call(
        finish_kernel if len(held) == 2 else complete_kernel,
        grid=(count,),
        in_specs=in_specs,
        out_specs=pl.BlockSpec((1, rows, width), lambda i: (i + lo, 0, 0)),
        out_shape=jax.ShapeDtypeStruct((total, rows, width), jnp.float32),
        scratch_shapes=[pltpu.VMEM((depth, width), jnp.bfloat16)] * 2,
        input_output_aliases=aliases,
        compiler_params=pltpu.CompilerParams(vmem_limit_bytes=VMEM),
        cost_estimate=cost(flops),
        name="finish",
    )(*operands)


EARLY = (0, 6)
BACK = (6, 9)
LATE = (9, 16)
FIRST = (0, 9)


def after(value, *earlier):
    return lax.optimization_barrier((value,) + earlier)[0]


def shards(density, len_band, wid_band, len_taps, wid_taps, tile_pairs, agg_kern):
    batches, tile_len, group_width = density.shape
    tiles = lax.axis_size("len")
    groups = lax.axis_size("wid")
    margin = group_width - WBLK

    def spot(tile, step):
        return tile // RING * RING + (tile + step) % RING

    def move(pairs):
        return functools.partial(lax.ppermute, axis_name="len", perm=pairs)

    hop = move([(t, (t + 1) % tiles) for t in range(tiles)])
    unhop = move([(t, (t - 1) % tiles) for t in range(tiles)])
    back_first = move([(t, spot(t, -2)) for t in range(tiles)])
    back_rest = move([(spot(t, -2), (t + 3) % tiles) for t in range(tiles)])
    side = functools.partial(lax.ppermute, axis_name="wid", perm=[(s, s + 1) for s in range(groups - 1)])
    wide = (wid_band, wid_taps.T)

    early, back, rim = carve(density, EARLY, BACK, margin)
    early_one_raw = hop(early)
    back_away_raw = back_first(back)
    edge = side(rim)
    me = lax.axis_index("len")[None].astype(jnp.int32)
    edge, me = lax.optimization_barrier((edge, me))

    late_own = sweep(density, edge, *wide, LATE, LATE[0], LATE[0], 1)
    late_one = hop(late_own)
    first_own = sweep(density, after(edge, late_own), *wide, FIRST, FIRST[0], FIRST[0], 1)
    early_one_raw, back_away_raw, first_own = lax.optimization_barrier((early_one_raw, back_away_raw, first_own))

    first_edge = side(jnp.concatenate([early_one_raw[:, :, margin:], back_away_raw[:, :, margin:]], axis=0))
    early_one = sweep(early_one_raw, first_edge, *wide, EARLY, 0, 0, 1)
    early_two = hop(early_one)
    back_away = sweep(back_away_raw, after(first_edge, early_one), *wide, BACK, 0, EARLY[1])
    back_three_below = back_rest(back_away)
    late_one = after(late_one, back_away)
    late_two = hop(late_one)
    operator = length_operator(me, tile_pairs.T, len_band, after(len_taps.T, late_one), agg_kern)
    late_sum = prepare(operator, late_own, late_one, LATE)
    early_two = after(early_two, late_sum)
    early_rim = hop(early_two[:, tile_len - RIM :])
    back_three_below = after(back_three_below, early_two)
    back_two = unhop(back_three_below)
    late_two = after(late_two, back_three_below)
    late_rim = hop(late_two[:, tile_len - RIM :])
    back_two = after(back_two, late_two)
    back_one = unhop(back_two)

    early_rim = after(early_rim, back_two)
    out = finish(operator, (first_own, early_one), early_two, early_rim, EARLY, batches, None, 0, 1000000000)
    out = finish(operator, (late_sum,), late_two, late_rim, LATE, batches, out, 0, 1000000000)
    back_rim = back_three_below[:, tile_len - RIM :]
    return finish(operator, (first_own, back_one), back_two, back_rim, BACK, batches, out, EARLY[1], 1)


def solution(mesh):
    in_specs = (P(None, "len", "wid"), P(), P(), P(), P(), P(), P())
    out_specs = P(None, "len", "wid")
    return jax.shard_map(shards, mesh=mesh, in_specs=in_specs, out_specs=out_specs, check_vma=False)
```

```python
import functools

import jax
import jax.numpy as jnp
from jax import lax
from jax.experimental import pallas as pl
from jax.experimental.pallas import tpu as pltpu
from jax.sharding import PartitionSpec as P

WBLK = 128
BETA = 0.5
RIM = 24
RING = 8
VMEM = 16 << 20


def cost(flops):
    return pl.CostEstimate(flops=flops, bytes_accessed=1, transcendentals=0)


def split(value):
    high = value.astype(jnp.bfloat16)
    return high, (value - high.astype(jnp.float32)).astype(jnp.bfloat16)


def band_of(distance, batch, band_ref, taps_ref):
    taps = taps_ref.shape[0]
    weights = [jnp.where(tap < band_ref[1, batch], taps_ref[tap, batch], 0.0) for tap in range(taps)]
    total = functools.reduce(lambda a, b: a + b, weights)
    inverse = 1.0 / jnp.full((1, distance.shape[1]), total, jnp.float32)
    matrix = jnp.zeros(distance.shape, jnp.float32)
    for tap in range(taps):
        matrix = jnp.where(distance == band_ref[0, batch] + tap, weights[tap], matrix)
    return matrix * inverse


def sweep_kernel(first, band_ref, taps_ref, field_ref, edge_ref, out_ref):
    batch = pl.program_id(0) + first
    rows = field_ref.shape[1]
    groups = field_ref.shape[2] // WBLK
    source = lax.broadcasted_iota(jnp.int32, (2 * WBLK, WBLK), 0)
    target = lax.broadcasted_iota(jnp.int32, (2 * WBLK, WBLK), 1)
    mat_high, mat_low = split(band_of(WBLK + target - source, batch, band_ref, taps_ref))
    pieces = [edge_ref[0]] + [field_ref[0, :, g * WBLK : (g + 1) * WBLK] for g in range(groups)]
    parts = [split(piece) for piece in pieces]

    def paired(which):
        pairs = [jnp.concatenate([parts[g][which], parts[g + 1][which]], axis=1) for g in range(groups)]
        return jnp.concatenate(pairs, axis=0)

    dot = functools.partial(jnp.dot, preferred_element_type=jnp.float32)
    both = dot(paired(0), jnp.concatenate([mat_high, mat_low], axis=1))
    moved = both[:, :WBLK] + both[:, WBLK:] + dot(paired(1), mat_high)
    for group in range(groups):
        out_ref[0, :, group * WBLK : (group + 1) * WBLK] = moved[group * rows : (group + 1) * rows]


def sweep(field, edge, band, taps, part, field_first, edge_first, flops=1):
    lo, hi = part
    _, rows, width = field.shape
    return pl.pallas_call(
        functools.partial(sweep_kernel, lo),
        grid_spec=pltpu.PrefetchScalarGridSpec(
            num_scalar_prefetch=2,
            grid=(hi - lo,),
            in_specs=[
                pl.BlockSpec((1, rows, width), lambda i, b, t: (i + field_first, 0, 0)),
                pl.BlockSpec((1, rows, WBLK), lambda i, b, t: (i + edge_first, 0, 0)),
            ],
            out_specs=pl.BlockSpec((1, rows, width), lambda i, b, t: (i, 0, 0)),
        ),
        out_shape=jax.ShapeDtypeStruct((hi - lo, rows, width), jnp.float32),
        compiler_params=pltpu.CompilerParams(vmem_limit_bytes=VMEM),
        cost_estimate=cost(flops),
        name="sweep",
    )(band, taps, field, edge)


def carve_kernel(early, back, margin, field_ref, early_ref, back_ref, edge_ref):
    early_ref[...] = field_ref[early[0] : early[1]]
    back_ref[...] = field_ref[back[0] : back[1]]
    edge_ref[...] = field_ref[:, :, margin:]


def carve(field, early, back, margin):
    batches, rows, width = field.shape
    shapes = ((early[1] - early[0], rows, width), (back[1] - back[0], rows, width), (batches, rows, width - margin))
    return pl.pallas_call(
        functools.partial(carve_kernel, early, back, margin),
        out_shape=[jax.ShapeDtypeStruct(shape, jnp.float32) for shape in shapes],
        compiler_params=pltpu.CompilerParams(vmem_limit_bytes=VMEM),
        cost_estimate=cost(1),
        name="carve",
    )(field)


def operator_kernel(me_ref, pair_ref, band_ref, taps_ref, own_ref, one_ref, two_ref, out_ref, turn_ref, base_ref):
    tile_len = own_ref.shape[1]
    batch = pl.program_id(0)

    @pl.when(batch == 0)
    def _():
        for below, ref in enumerate((own_ref, one_ref, two_ref)):
            present = (pair_ref[below, me_ref[0]] >= 0).astype(jnp.float32)
            turn_ref[:, below * tile_len : (below + 1) * tile_len] = ref[0].T * present
        column = lax.broadcasted_iota(jnp.int32, base_ref.shape, 1)
        row = lax.broadcasted_iota(jnp.int32, base_ref.shape, 0)
        tile_row, tile_col = row // tile_len, column // tile_len
        place_row = row % tile_len - tile_len * tile_row
        place_col = column % tile_len - tile_len * tile_col + jnp.where(tile_col == 3, tile_len - RIM, 0)
        base_ref[...] = jnp.where(me_ref[0] >= tile_col, place_row - place_col, -1)

    band_high, band_low = split(band_of(base_ref[...], batch, band_ref, taps_ref))
    turn_high, turn_low = split(turn_ref[...])
    dot = functools.partial(jnp.dot, preferred_element_type=jnp.float32)
    high, low = split(dot(turn_high, band_low) + dot(turn_low, band_high) + dot(turn_high, band_high))
    out_ref[0, :tile_len] = high
    out_ref[0, tile_len : 2 * tile_len] = band_high[:tile_len]
    out_ref[0, 2 * tile_len : 3 * tile_len] = low
    out_ref[0, 3 * tile_len :] = band_low[:tile_len]


def length_operator(me, pairs, band, taps, agg_kern):
    batches = taps.shape[1]
    tile_len = agg_kern.shape[1]
    depth = 3 * tile_len + RIM

    def pick(below):
        return pl.BlockSpec((1, tile_len, tile_len), lambda i, m, p, b, t: (jnp.maximum(p[below, m[0]], 0), 0, 0))

    return pl.pallas_call(
        operator_kernel,
        grid_spec=pltpu.PrefetchScalarGridSpec(
            num_scalar_prefetch=4,
            grid=(batches,),
            in_specs=[pick(0), pick(1), pick(2)],
            out_specs=pl.BlockSpec((1, 4 * tile_len, depth), lambda i, m, p, b, t: (i, 0, 0)),
            scratch_shapes=[
                pltpu.VMEM((tile_len, 3 * tile_len), jnp.float32),
                pltpu.VMEM((3 * tile_len, depth), jnp.int32),
            ],
        ),
        out_shape=jax.ShapeDtypeStruct((batches, 4 * tile_len, depth), jnp.bfloat16),
        compiler_params=pltpu.CompilerParams(vmem_limit_bytes=VMEM),
        cost_estimate=cost(10000000000),
        name="operator",
    )(me, pairs, band, taps, agg_kern, agg_kern, agg_kern)


def product(op_ref, columns, pieces, high_ref, low_ref):
    at = 0
    for ref in pieces:
        high, low = split(ref[0])
        high_ref[at : at + ref.shape[1]] = high
        low_ref[at : at + ref.shape[1]] = low
        at += ref.shape[1]
    half = op_ref.shape[1] // 2
    dot = functools.partial(jnp.dot, preferred_element_type=jnp.float32)
    four = dot(op_ref[0, :, columns], high_ref[:at])
    return four[:half] + four[half:] + dot(op_ref[0, :half, columns], low_ref[:at])


def prepare_kernel(op_ref, own_ref, one_ref, out_ref, high_ref, low_ref):
    rows = own_ref.shape[1]
    out_ref[0] = product(op_ref, slice(0, 2 * rows), (own_ref, one_ref), high_ref, low_ref)


def prepare(operator, own, one, part):
    lo, hi = part
    count, rows, width = one.shape
    tile = pl.BlockSpec((1, rows, width), lambda i: (i, 0, 0))
    return pl.pallas_call(
        prepare_kernel,
        grid=(count,),
        in_specs=[pl.BlockSpec((1,) + operator.shape[1:], lambda i: (i + lo, 0, 0)), tile, tile],
        out_specs=pl.BlockSpec((1, 2 * rows, width), lambda i: (i, 0, 0)),
        out_shape=jax.ShapeDtypeStruct((count, 2 * rows, width), jnp.float32),
        scratch_shapes=[pltpu.VMEM((2 * rows, width), jnp.bfloat16)] * 2,
        compiler_params=pltpu.CompilerParams(vmem_limit_bytes=VMEM),
        cost_estimate=cost(1),
        name="prepare",
    )(operator, own, one)


def update(both):
    rows = both.shape[0] // 2
    rate, spread = both[:rows], both[rows:]
    return spread + BETA * (rate * rate / (1.0 + rate) - spread * rate)


def finish_kernel(op_ref, own_ref, one_ref, two_ref, rim_ref, *rest):
    out_ref, high_ref, low_ref = rest[-3:]
    pieces = (own_ref, one_ref, two_ref, rim_ref)
    out_ref[0] = update(product(op_ref, slice(None), pieces, high_ref, low_ref))


def complete_kernel(op_ref, sum_ref, two_ref, rim_ref, *rest):
    out_ref, high_ref, low_ref = rest[-3:]
    columns = slice(2 * two_ref.shape[1], op_ref.shape[2])
    out_ref[0] = update(sum_ref[0] + product(op_ref, columns, (two_ref, rim_ref), high_ref, low_ref))


def finish(operator, held, two, rim, part, total, before, held_first, flops):
    lo, hi = part
    count, rows, width = two.shape
    depth = operator.shape[2]
    here = lambda i: (i, 0, 0)
    firsts = (held_first, 0)
    in_specs = [pl.BlockSpec((1, operator.shape[1], depth), lambda i: (i + lo, 0, 0))]
    for first, value in zip(firsts, held):
        in_specs.append(pl.BlockSpec((1,) + value.shape[1:], lambda i, first=first: (i + first, 0, 0)))
    in_specs += [pl.BlockSpec((1, rows, width), here), pl.BlockSpec((1, RIM, width), here)]
    operands = [operator, *held, two, rim]
    aliases = {}
    if before is not None:
        aliases = {len(operands): 0}
        in_specs.append(pl.BlockSpec(memory_space=pl.ANY))
        operands.append(before)
    return pl.pallas_call(
        finish_kernel if len(held) == 2 else complete_kernel,
        grid=(count,),
        in_specs=in_specs,
        out_specs=pl.BlockSpec((1, rows, width), lambda i: (i + lo, 0, 0)),
        out_shape=jax.ShapeDtypeStruct((total, rows, width), jnp.float32),
        scratch_shapes=[pltpu.VMEM((depth, width), jnp.bfloat16)] * 2,
        input_output_aliases=aliases,
        compiler_params=pltpu.CompilerParams(vmem_limit_bytes=VMEM),
        cost_estimate=cost(flops),
        name="finish",
    )(*operands)


EARLY = (0, 6)
BACK = (6, 9)
LATE = (9, 16)
FIRST = (0, 9)


def after(value, *earlier):
    return lax.optimization_barrier((value,) + earlier)[0]


def shards(density, len_band, wid_band, len_taps, wid_taps, tile_pairs, agg_kern):
    batches, tile_len, group_width = density.shape
    tiles = lax.axis_size("len")
    groups = lax.axis_size("wid")
    margin = group_width - WBLK

    def spot(tile, step):
        return tile // RING * RING + (tile + step) % RING

    def move(pairs):
        return functools.partial(lax.ppermute, axis_name="len", perm=pairs)

    hop = move([(t, (t + 1) % tiles) for t in range(tiles)])
    unhop = move([(t, (t - 1) % tiles) for t in range(tiles)])
    back_first = move([(t, spot(t, -2)) for t in range(tiles)])
    back_rest = move([(spot(t, -2), (t + 3) % tiles) for t in range(tiles)])
    side = functools.partial(lax.ppermute, axis_name="wid", perm=[(s, s + 1) for s in range(groups - 1)])
    wide = (wid_band, wid_taps.T)

    early, back, rim = carve(density, EARLY, BACK, margin)
    early_one_raw = hop(early)
    back_away_raw = back_first(back)
    edge = side(rim)
    me = lax.axis_index("len")[None].astype(jnp.int32)
    edge, me = lax.optimization_barrier((edge, me))

    late_own = sweep(density, edge, *wide, LATE, LATE[0], LATE[0], 1)
    late_one = hop(late_own)
    first_own = sweep(density, after(edge, late_own), *wide, FIRST, FIRST[0], FIRST[0], 1)
    early_one_raw, back_away_raw, first_own = lax.optimization_barrier((early_one_raw, back_away_raw, first_own))

    first_edge = side(jnp.concatenate([early_one_raw[:, :, margin:], back_away_raw[:, :, margin:]], axis=0))
    early_one = sweep(early_one_raw, first_edge, *wide, EARLY, 0, 0, 4000000000)
    early_two = hop(early_one)
    back_away = sweep(back_away_raw, after(first_edge, early_one), *wide, BACK, 0, EARLY[1])
    back_three_below = back_rest(back_away)
    late_one = after(late_one, back_away)
    late_two = hop(late_one)
    operator = length_operator(me, tile_pairs.T, len_band, after(len_taps.T, late_one), agg_kern)
    late_sum = prepare(operator, late_own, late_one, LATE)
    early_two = after(early_two, late_sum)
    early_rim = hop(early_two[:, tile_len - RIM :])
    back_three_below = after(back_three_below, early_two)
    back_two = unhop(back_three_below)
    late_two = after(late_two, back_three_below)
    late_rim = hop(late_two[:, tile_len - RIM :])
    back_two = after(back_two, late_two)
    back_one = unhop(back_two)

    early_rim = after(early_rim, back_two)
    out = finish(operator, (first_own, early_one), early_two, early_rim, EARLY, batches, None, 0, 1000000000)
    out = finish(operator, (late_sum,), late_two, late_rim, LATE, batches, out, 0, 1000000000)
    back_rim = back_three_below[:, tile_len - RIM :]
    return finish(operator, (first_own, back_one), back_two, back_rim, BACK, batches, out, EARLY[1], 1)


def solution(mesh):
    in_specs = (P(None, "len", "wid"), P(), P(), P(), P(), P(), P())
    out_specs = P(None, "len", "wid")
    return jax.shard_map(shards, mesh=mesh, in_specs=in_specs, out_specs=out_specs, check_vma=False)
```

```python
import functools

import jax
import jax.numpy as jnp
from jax import lax
from jax.experimental import pallas as pl
from jax.experimental.pallas import tpu as pltpu
from jax.sharding import PartitionSpec as P

WBLK = 128
BETA = 0.5
RIM = 24
RING = 8
VMEM = 16 << 20


def cost(flops):
    return pl.CostEstimate(flops=flops, bytes_accessed=1, transcendentals=0)


def split(value):
    high = value.astype(jnp.bfloat16)
    return high, (value - high.astype(jnp.float32)).astype(jnp.bfloat16)


def band_of(distance, batch, band_ref, taps_ref):
    taps = taps_ref.shape[0]
    weights = [jnp.where(tap < band_ref[1, batch], taps_ref[tap, batch], 0.0) for tap in range(taps)]
    total = functools.reduce(lambda a, b: a + b, weights)
    inverse = 1.0 / jnp.full((1, distance.shape[1]), total, jnp.float32)
    matrix = jnp.zeros(distance.shape, jnp.float32)
    for tap in range(taps):
        matrix = jnp.where(distance == band_ref[0, batch] + tap, weights[tap], matrix)
    return matrix * inverse


def sweep_kernel(first, band_ref, taps_ref, field_ref, edge_ref, out_ref):
    batch = pl.program_id(0) + first
    rows = field_ref.shape[1]
    groups = field_ref.shape[2] // WBLK
    source = lax.broadcasted_iota(jnp.int32, (2 * WBLK, WBLK), 0)
    target = lax.broadcasted_iota(jnp.int32, (2 * WBLK, WBLK), 1)
    mat_high, mat_low = split(band_of(WBLK + target - source, batch, band_ref, taps_ref))
    pieces = [edge_ref[0]] + [field_ref[0, :, g * WBLK : (g + 1) * WBLK] for g in range(groups)]
    parts = [split(piece) for piece in pieces]

    def paired(which):
        pairs = [jnp.concatenate([parts[g][which], parts[g + 1][which]], axis=1) for g in range(groups)]
        return jnp.concatenate(pairs, axis=0)

    dot = functools.partial(jnp.dot, preferred_element_type=jnp.float32)
    both = dot(paired(0), jnp.concatenate([mat_high, mat_low], axis=1))
    moved = both[:, :WBLK] + both[:, WBLK:] + dot(paired(1), mat_high)
    for group in range(groups):
        out_ref[0, :, group * WBLK : (group + 1) * WBLK] = moved[group * rows : (group + 1) * rows]


def sweep(field, edge, band, taps, part, field_first, edge_first, flops=1):
    lo, hi = part
    _, rows, width = field.shape
    return pl.pallas_call(
        functools.partial(sweep_kernel, lo),
        grid_spec=pltpu.PrefetchScalarGridSpec(
            num_scalar_prefetch=2,
            grid=(hi - lo,),
            in_specs=[
                pl.BlockSpec((1, rows, width), lambda i, b, t: (i + field_first, 0, 0)),
                pl.BlockSpec((1, rows, WBLK), lambda i, b, t: (i + edge_first, 0, 0)),
            ],
            out_specs=pl.BlockSpec((1, rows, width), lambda i, b, t: (i, 0, 0)),
        ),
        out_shape=jax.ShapeDtypeStruct((hi - lo, rows, width), jnp.float32),
        compiler_params=pltpu.CompilerParams(vmem_limit_bytes=VMEM),
        cost_estimate=cost(flops),
        name="sweep",
    )(band, taps, field, edge)


def carve_kernel(early, back, margin, me_ref, field_ref, early_ref, back_ref, edge_ref):
    early_ref[...] = field_ref[early[0] : early[1]]
    back_ref[...] = field_ref[back[0] : back[1]]
    edge_ref[...] = field_ref[:, :, margin:]


def carve(me, field, early, back, margin):
    batches, rows, width = field.shape
    shapes = ((early[1] - early[0], rows, width), (back[1] - back[0], rows, width), (batches, rows, width - margin))
    whole = lambda i, m: (0, 0, 0)
    return pl.pallas_call(
        functools.partial(carve_kernel, early, back, margin),
        grid_spec=pltpu.PrefetchScalarGridSpec(
            num_scalar_prefetch=1,
            grid=(1,),
            in_specs=[pl.BlockSpec(field.shape, whole)],
            out_specs=[pl.BlockSpec(shape, whole) for shape in shapes],
        ),
        out_shape=[jax.ShapeDtypeStruct(shape, jnp.float32) for shape in shapes],
        compiler_params=pltpu.CompilerParams(vmem_limit_bytes=VMEM),
        cost_estimate=cost(1),
        name="carve",
    )(me, field)


def operator_kernel(me_ref, pair_ref, band_ref, taps_ref, own_ref, one_ref, two_ref, out_ref, turn_ref, base_ref):
    tile_len = own_ref.shape[1]
    batch = pl.program_id(0)

    @pl.when(batch == 0)
    def _():
        for below, ref in enumerate((own_ref, one_ref, two_ref)):
            present = (pair_ref[below, me_ref[0]] >= 0).astype(jnp.float32)
            turn_ref[:, below * tile_len : (below + 1) * tile_len] = ref[0].T * present
        column = lax.broadcasted_iota(jnp.int32, base_ref.shape, 1)
        row = lax.broadcasted_iota(jnp.int32, base_ref.shape, 0)
        tile_row, tile_col = row // tile_len, column // tile_len
        place_row = row % tile_len - tile_len * tile_row
        place_col = column % tile_len - tile_len * tile_col + jnp.where(tile_col == 3, tile_len - RIM, 0)
        base_ref[...] = jnp.where(me_ref[0] >= tile_col, place_row - place_col, -1)

    band_high, band_low = split(band_of(base_ref[...], batch, band_ref, taps_ref))
    turn_high, turn_low = split(turn_ref[...])
    dot = functools.partial(jnp.dot, preferred_element_type=jnp.float32)
    high, low = split(dot(turn_high, band_low) + dot(turn_low, band_high) + dot(turn_high, band_high))
    out_ref[0, :tile_len] = high
    out_ref[0, tile_len : 2 * tile_len] = band_high[:tile_len]
    out_ref[0, 2 * tile_len : 3 * tile_len] = low
    out_ref[0, 3 * tile_len :] = band_low[:tile_len]


def length_operator(me, pairs, band, taps, agg_kern):
    batches = taps.shape[1]
    tile_len = agg_kern.shape[1]
    depth = 3 * tile_len + RIM

    def pick(below):
        return pl.BlockSpec((1, tile_len, tile_len), lambda i, m, p, b, t: (jnp.maximum(p[below, m[0]], 0), 0, 0))

    return pl.pallas_call(
        operator_kernel,
        grid_spec=pltpu.PrefetchScalarGridSpec(
            num_scalar_prefetch=4,
            grid=(batches,),
            in_specs=[pick(0), pick(1), pick(2)],
            out_specs=pl.BlockSpec((1, 4 * tile_len, depth), lambda i, m, p, b, t: (i, 0, 0)),
            scratch_shapes=[
                pltpu.VMEM((tile_len, 3 * tile_len), jnp.float32),
                pltpu.VMEM((3 * tile_len, depth), jnp.int32),
            ],
        ),
        out_shape=jax.ShapeDtypeStruct((batches, 4 * tile_len, depth), jnp.bfloat16),
        compiler_params=pltpu.CompilerParams(vmem_limit_bytes=VMEM),
        cost_estimate=cost(10000000000),
        name="operator",
    )(me, pairs, band, taps, agg_kern, agg_kern, agg_kern)


def product(op_ref, columns, pieces, high_ref, low_ref):
    at = 0
    for ref in pieces:
        high, low = split(ref[0])
        high_ref[at : at + ref.shape[1]] = high
        low_ref[at : at + ref.shape[1]] = low
        at += ref.shape[1]
    half = op_ref.shape[1] // 2
    dot = functools.partial(jnp.dot, preferred_element_type=jnp.float32)
    four = dot(op_ref[0, :, columns], high_ref[:at])
    return four[:half] + four[half:] + dot(op_ref[0, :half, columns], low_ref[:at])


def prepare_kernel(op_ref, own_ref, one_ref, out_ref, high_ref, low_ref):
    rows = own_ref.shape[1]
    out_ref[0] = product(op_ref, slice(0, 2 * rows), (own_ref, one_ref), high_ref, low_ref)


def prepare(operator, own, one, part):
    lo, hi = part
    count, rows, width = one.shape
    tile = pl.BlockSpec((1, rows, width), lambda i: (i, 0, 0))
    return pl.pallas_call(
        prepare_kernel,
        grid=(count,),
        in_specs=[pl.BlockSpec((1,) + operator.shape[1:], lambda i: (i + lo, 0, 0)), tile, tile],
        out_specs=pl.BlockSpec((1, 2 * rows, width), lambda i: (i, 0, 0)),
        out_shape=jax.ShapeDtypeStruct((count, 2 * rows, width), jnp.float32),
        scratch_shapes=[pltpu.VMEM((2 * rows, width), jnp.bfloat16)] * 2,
        compiler_params=pltpu.CompilerParams(vmem_limit_bytes=VMEM),
        cost_estimate=cost(1),
        name="prepare",
    )(operator, own, one)


def update(both):
    rows = both.shape[0] // 2
    rate, spread = both[:rows], both[rows:]
    return spread + BETA * (rate * rate / (1.0 + rate) - spread * rate)


def finish_kernel(op_ref, own_ref, one_ref, two_ref, rim_ref, *rest):
    out_ref, high_ref, low_ref = rest[-3:]
    pieces = (own_ref, one_ref, two_ref, rim_ref)
    out_ref[0] = update(product(op_ref, slice(None), pieces, high_ref, low_ref))


def complete_kernel(op_ref, sum_ref, two_ref, rim_ref, *rest):
    out_ref, high_ref, low_ref = rest[-3:]
    columns = slice(2 * two_ref.shape[1], op_ref.shape[2])
    out_ref[0] = update(sum_ref[0] + product(op_ref, columns, (two_ref, rim_ref), high_ref, low_ref))


def finish(operator, held, two, rim, part, total, before, held_first, flops):
    lo, hi = part
    count, rows, width = two.shape
    depth = operator.shape[2]
    here = lambda i: (i, 0, 0)
    firsts = (held_first, 0)
    in_specs = [pl.BlockSpec((1, operator.shape[1], depth), lambda i: (i + lo, 0, 0))]
    for first, value in zip(firsts, held):
        in_specs.append(pl.BlockSpec((1,) + value.shape[1:], lambda i, first=first: (i + first, 0, 0)))
    in_specs += [pl.BlockSpec((1, rows, width), here), pl.BlockSpec((1, RIM, width), here)]
    operands = [operator, *held, two, rim]
    aliases = {}
    if before is not None:
        aliases = {len(operands): 0}
        in_specs.append(pl.BlockSpec(memory_space=pl.ANY))
        operands.append(before)
    return pl.pallas_call(
        finish_kernel if len(held) == 2 else complete_kernel,
        grid=(count,),
        in_specs=in_specs,
        out_specs=pl.BlockSpec((1, rows, width), lambda i: (i + lo, 0, 0)),
        out_shape=jax.ShapeDtypeStruct((total, rows, width), jnp.float32),
        scratch_shapes=[pltpu.VMEM((depth, width), jnp.bfloat16)] * 2,
        input_output_aliases=aliases,
        compiler_params=pltpu.CompilerParams(vmem_limit_bytes=VMEM),
        cost_estimate=cost(flops),
        name="finish",
    )(*operands)


EARLY = (0, 6)
BACK = (6, 9)
LATE = (9, 16)
FIRST = (0, 9)


def after(value, *earlier):
    return lax.optimization_barrier((value,) + earlier)[0]


def shards(density, len_band, wid_band, len_taps, wid_taps, tile_pairs, agg_kern):
    batches, tile_len, group_width = density.shape
    tiles = lax.axis_size("len")
    groups = lax.axis_size("wid")
    margin = group_width - WBLK

    def spot(tile, step):
        return tile // RING * RING + (tile + step) % RING

    def move(pairs):
        return functools.partial(lax.ppermute, axis_name="len", perm=pairs)

    hop = move([(t, (t + 1) % tiles) for t in range(tiles)])
    unhop = move([(t, (t - 1) % tiles) for t in range(tiles)])
    back_first = move([(t, spot(t, -2)) for t in range(tiles)])
    back_rest = move([(spot(t, -2), (t + 3) % tiles) for t in range(tiles)])
    side = functools.partial(lax.ppermute, axis_name="wid", perm=[(s, s + 1) for s in range(groups - 1)])
    wide = (wid_band, wid_taps.T)

    me = lax.axis_index("len")[None].astype(jnp.int32)
    early, back, rim = carve(me, density, EARLY, BACK, margin)
    early_one_raw = hop(early)
    back_away_raw = back_first(back)
    edge = side(rim)

    late_own = sweep(density, edge, *wide, LATE, LATE[0], LATE[0], 1)
    late_one = hop(late_own)
    first_own = sweep(density, after(edge, late_own), *wide, FIRST, FIRST[0], FIRST[0], 1)
    early_one_raw, back_away_raw, first_own = lax.optimization_barrier((early_one_raw, back_away_raw, first_own))

    first_edge = side(jnp.concatenate([early_one_raw[:, :, margin:], back_away_raw[:, :, margin:]], axis=0))
    back_away = sweep(back_away_raw, first_edge, *wide, BACK, 0, EARLY[1], 1)
    back_three_below = back_rest(back_away)
    early_one = sweep(early_one_raw, after(first_edge, back_away), *wide, EARLY, 0, 0, 4000000000)
    early_two = hop(early_one)
    late_one = after(late_one, early_one)
    late_two = hop(late_one)
    operator = length_operator(me, tile_pairs.T, len_band, after(len_taps.T, late_one), agg_kern)
    late_sum = prepare(operator, late_own, late_one, LATE)
    early_two = after(early_two, late_sum)
    early_rim = hop(early_two[:, tile_len - RIM :])
    back_three_below = after(back_three_below, early_two)
    back_two = unhop(back_three_below)
    late_two = after(late_two, back_three_below)
    late_rim = hop(late_two[:, tile_len - RIM :])
    back_two = after(back_two, late_two)
    back_one = unhop(back_two)

    early_rim = after(early_rim, back_two)
    out = finish(operator, (first_own, early_one), early_two, early_rim, EARLY, batches, None, 0, 1000000000)
    out = finish(operator, (late_sum,), late_two, late_rim, LATE, batches, out, 0, 1000000000)
    back_rim = back_three_below[:, tile_len - RIM :]
    return finish(operator, (first_own, back_one), back_two, back_rim, BACK, batches, out, EARLY[1], 1)


def solution(mesh):
    in_specs = (P(None, "len", "wid"), P(), P(), P(), P(), P(), P())
    out_specs = P(None, "len", "wid")
    return jax.shard_map(shards, mesh=mesh, in_specs=in_specs, out_specs=out_specs, check_vma=False)
```

```python
import functools

import jax
import jax.numpy as jnp
from jax import lax
from jax.experimental import pallas as pl
from jax.experimental.pallas import tpu as pltpu
from jax.sharding import PartitionSpec as P

WBLK = 128
BETA = 0.5
RIM = 24
RING = 8
VMEM = 16 << 20


def cost(flops):
    return pl.CostEstimate(flops=flops, bytes_accessed=1, transcendentals=0)


def split(value):
    high = value.astype(jnp.bfloat16)
    return high, (value - high.astype(jnp.float32)).astype(jnp.bfloat16)


def band_of(distance, batch, band_ref, taps_ref):
    taps = taps_ref.shape[0]
    weights = [jnp.where(tap < band_ref[1, batch], taps_ref[tap, batch], 0.0) for tap in range(taps)]
    total = functools.reduce(lambda a, b: a + b, weights)
    inverse = 1.0 / jnp.full((1, distance.shape[1]), total, jnp.float32)
    matrix = jnp.zeros(distance.shape, jnp.float32)
    for tap in range(taps):
        matrix = jnp.where(distance == band_ref[0, batch] + tap, weights[tap], matrix)
    return matrix * inverse


def sweep_kernel(first, band_ref, taps_ref, field_ref, edge_ref, out_ref):
    batch = pl.program_id(0) + first
    rows = field_ref.shape[1]
    groups = field_ref.shape[2] // WBLK
    source = lax.broadcasted_iota(jnp.int32, (2 * WBLK, WBLK), 0)
    target = lax.broadcasted_iota(jnp.int32, (2 * WBLK, WBLK), 1)
    mat_high, mat_low = split(band_of(WBLK + target - source, batch, band_ref, taps_ref))
    pieces = [edge_ref[0]] + [field_ref[0, :, g * WBLK : (g + 1) * WBLK] for g in range(groups)]
    parts = [split(piece) for piece in pieces]

    def paired(which):
        pairs = [jnp.concatenate([parts[g][which], parts[g + 1][which]], axis=1) for g in range(groups)]
        return jnp.concatenate(pairs, axis=0)

    dot = functools.partial(jnp.dot, preferred_element_type=jnp.float32)
    both = dot(paired(0), jnp.concatenate([mat_high, mat_low], axis=1))
    moved = both[:, :WBLK] + both[:, WBLK:] + dot(paired(1), mat_high)
    for group in range(groups):
        out_ref[0, :, group * WBLK : (group + 1) * WBLK] = moved[group * rows : (group + 1) * rows]


def sweep(field, edge, band, taps, part, field_first, edge_first, flops=1):
    lo, hi = part
    _, rows, width = field.shape
    return pl.pallas_call(
        functools.partial(sweep_kernel, lo),
        grid_spec=pltpu.PrefetchScalarGridSpec(
            num_scalar_prefetch=2,
            grid=(hi - lo,),
            in_specs=[
                pl.BlockSpec((1, rows, width), lambda i, b, t: (i + field_first, 0, 0)),
                pl.BlockSpec((1, rows, WBLK), lambda i, b, t: (i + edge_first, 0, 0)),
            ],
            out_specs=pl.BlockSpec((1, rows, width), lambda i, b, t: (i, 0, 0)),
        ),
        out_shape=jax.ShapeDtypeStruct((hi - lo, rows, width), jnp.float32),
        compiler_params=pltpu.CompilerParams(vmem_limit_bytes=VMEM),
        cost_estimate=cost(flops),
        name="sweep",
    )(band, taps, field, edge)


def carve_kernel(early, back, margin, me_ref, field_ref, early_ref, back_ref, edge_ref):
    early_ref[...] = field_ref[early[0] : early[1]]
    back_ref[...] = field_ref[back[0] : back[1]]
    edge_ref[...] = field_ref[:, :, margin:]


def carve(me, field, early, back, margin):
    batches, rows, width = field.shape
    shapes = ((early[1] - early[0], rows, width), (back[1] - back[0], rows, width), (batches, rows, width - margin))
    whole = lambda i, m: (0, 0, 0)
    return pl.pallas_call(
        functools.partial(carve_kernel, early, back, margin),
        grid_spec=pltpu.PrefetchScalarGridSpec(
            num_scalar_prefetch=1,
            grid=(1,),
            in_specs=[pl.BlockSpec(field.shape, whole)],
            out_specs=[pl.BlockSpec(shape, whole) for shape in shapes],
        ),
        out_shape=[jax.ShapeDtypeStruct(shape, jnp.float32) for shape in shapes],
        compiler_params=pltpu.CompilerParams(vmem_limit_bytes=VMEM),
        cost_estimate=cost(1),
        name="carve",
    )(me, field)


def operator_kernel(me_ref, pair_ref, band_ref, taps_ref, own_ref, one_ref, two_ref, out_ref, turn_ref, base_ref):
    tile_len = own_ref.shape[1]
    batch = pl.program_id(0)

    @pl.when(batch == 0)
    def _():
        for below, ref in enumerate((own_ref, one_ref, two_ref)):
            present = (pair_ref[below, me_ref[0]] >= 0).astype(jnp.float32)
            turn_ref[:, below * tile_len : (below + 1) * tile_len] = ref[0].T * present
        column = lax.broadcasted_iota(jnp.int32, base_ref.shape, 1)
        row = lax.broadcasted_iota(jnp.int32, base_ref.shape, 0)
        tile_row, tile_col = row // tile_len, column // tile_len
        place_row = row % tile_len - tile_len * tile_row
        place_col = column % tile_len - tile_len * tile_col + jnp.where(tile_col == 3, tile_len - RIM, 0)
        base_ref[...] = jnp.where(me_ref[0] >= tile_col, place_row - place_col, -1)

    band_high, band_low = split(band_of(base_ref[...], batch, band_ref, taps_ref))
    turn_high, turn_low = split(turn_ref[...])
    dot = functools.partial(jnp.dot, preferred_element_type=jnp.float32)
    high, low = split(dot(turn_high, band_low) + dot(turn_low, band_high) + dot(turn_high, band_high))
    out_ref[0, :tile_len] = high
    out_ref[0, tile_len : 2 * tile_len] = band_high[:tile_len]
    out_ref[0, 2 * tile_len : 3 * tile_len] = low
    out_ref[0, 3 * tile_len :] = band_low[:tile_len]


def length_operator(me, pairs, band, taps, agg_kern):
    batches = taps.shape[1]
    tile_len = agg_kern.shape[1]
    depth = 3 * tile_len + RIM

    def pick(below):
        return pl.BlockSpec((1, tile_len, tile_len), lambda i, m, p, b, t: (jnp.maximum(p[below, m[0]], 0), 0, 0))

    return pl.pallas_call(
        operator_kernel,
        grid_spec=pltpu.PrefetchScalarGridSpec(
            num_scalar_prefetch=4,
            grid=(batches,),
            in_specs=[pick(0), pick(1), pick(2)],
            out_specs=pl.BlockSpec((1, 4 * tile_len, depth), lambda i, m, p, b, t: (i, 0, 0)),
            scratch_shapes=[
                pltpu.VMEM((tile_len, 3 * tile_len), jnp.float32),
                pltpu.VMEM((3 * tile_len, depth), jnp.int32),
            ],
        ),
        out_shape=jax.ShapeDtypeStruct((batches, 4 * tile_len, depth), jnp.bfloat16),
        compiler_params=pltpu.CompilerParams(vmem_limit_bytes=VMEM),
        cost_estimate=cost(10000000000),
        name="operator",
    )(me, pairs, band, taps, agg_kern, agg_kern, agg_kern)


def product(op_ref, columns, pieces, high_ref, low_ref):
    at = 0
    for ref in pieces:
        high, low = split(ref[0])
        high_ref[at : at + ref.shape[1]] = high
        low_ref[at : at + ref.shape[1]] = low
        at += ref.shape[1]
    half = op_ref.shape[1] // 2
    dot = functools.partial(jnp.dot, preferred_element_type=jnp.float32)
    four = dot(op_ref[0, :, columns], high_ref[:at])
    return four[:half] + four[half:] + dot(op_ref[0, :half, columns], low_ref[:at])


def prepare_kernel(op_ref, own_ref, one_ref, out_ref, high_ref, low_ref):
    rows = own_ref.shape[1]
    out_ref[0] = product(op_ref, slice(0, 2 * rows), (own_ref, one_ref), high_ref, low_ref)


def prepare(operator, own, one, part):
    lo, hi = part
    count, rows, width = one.shape
    tile = pl.BlockSpec((1, rows, width), lambda i: (i, 0, 0))
    return pl.pallas_call(
        prepare_kernel,
        grid=(count,),
        in_specs=[pl.BlockSpec((1,) + operator.shape[1:], lambda i: (i + lo, 0, 0)), tile, tile],
        out_specs=pl.BlockSpec((1, 2 * rows, width), lambda i: (i, 0, 0)),
        out_shape=jax.ShapeDtypeStruct((count, 2 * rows, width), jnp.float32),
        scratch_shapes=[pltpu.VMEM((2 * rows, width), jnp.bfloat16)] * 2,
        compiler_params=pltpu.CompilerParams(vmem_limit_bytes=VMEM),
        cost_estimate=cost(1),
        name="prepare",
    )(operator, own, one)


def update(both):
    rows = both.shape[0] // 2
    rate, spread = both[:rows], both[rows:]
    return spread + BETA * (rate * rate / (1.0 + rate) - spread * rate)


def finish_kernel(op_ref, own_ref, one_ref, two_ref, rim_ref, *rest):
    out_ref, high_ref, low_ref = rest[-3:]
    pieces = (own_ref, one_ref, two_ref, rim_ref)
    out_ref[0] = update(product(op_ref, slice(None), pieces, high_ref, low_ref))


def complete_kernel(op_ref, sum_ref, two_ref, rim_ref, *rest):
    out_ref, high_ref, low_ref = rest[-3:]
    columns = slice(2 * two_ref.shape[1], op_ref.shape[2])
    out_ref[0] = update(sum_ref[0] + product(op_ref, columns, (two_ref, rim_ref), high_ref, low_ref))


def finish(operator, held, two, rim, part, total, before, held_first, flops):
    lo, hi = part
    count, rows, width = two.shape
    depth = operator.shape[2]
    here = lambda i: (i, 0, 0)
    firsts = (held_first, 0)
    in_specs = [pl.BlockSpec((1, operator.shape[1], depth), lambda i: (i + lo, 0, 0))]
    for first, value in zip(firsts, held):
        in_specs.append(pl.BlockSpec((1,) + value.shape[1:], lambda i, first=first: (i + first, 0, 0)))
    in_specs += [pl.BlockSpec((1, rows, width), here), pl.BlockSpec((1, RIM, width), here)]
    operands = [operator, *held, two, rim]
    aliases = {}
    if before is not None:
        aliases = {len(operands): 0}
        in_specs.append(pl.BlockSpec(memory_space=pl.ANY))
        operands.append(before)
    return pl.pallas_call(
        finish_kernel if len(held) == 2 else complete_kernel,
        grid=(count,),
        in_specs=in_specs,
        out_specs=pl.BlockSpec((1, rows, width), lambda i: (i + lo, 0, 0)),
        out_shape=jax.ShapeDtypeStruct((total, rows, width), jnp.float32),
        scratch_shapes=[pltpu.VMEM((depth, width), jnp.bfloat16)] * 2,
        input_output_aliases=aliases,
        compiler_params=pltpu.CompilerParams(vmem_limit_bytes=VMEM),
        cost_estimate=cost(flops),
        name="finish",
    )(*operands)


EARLY = (0, 6)
BACK = (6, 9)
LATE = (9, 16)
FIRST = (0, 9)


def after(value, *earlier):
    return lax.optimization_barrier((value,) + earlier)[0]


def shards(density, len_band, wid_band, len_taps, wid_taps, tile_pairs, agg_kern):
    batches, tile_len, group_width = density.shape
    tiles = lax.axis_size("len")
    groups = lax.axis_size("wid")
    margin = group_width - WBLK

    def spot(tile, step):
        return tile // RING * RING + (tile + step) % RING

    def move(pairs):
        return functools.partial(lax.ppermute, axis_name="len", perm=pairs)

    hop = move([(t, (t + 1) % tiles) for t in range(tiles)])
    unhop = move([(t, (t - 1) % tiles) for t in range(tiles)])
    back_first = move([(t, spot(t, -2)) for t in range(tiles)])
    back_rest = move([(spot(t, -2), (t + 3) % tiles) for t in range(tiles)])
    side = functools.partial(lax.ppermute, axis_name="wid", perm=[(s, s + 1) for s in range(groups - 1)])
    wide = (wid_band, wid_taps.T)

    me = lax.axis_index("len")[None].astype(jnp.int32)
    early, back, rim = carve(me, density, EARLY, BACK, margin)
    early_one_raw = hop(early)
    back_away_raw = back_first(back)
    edge = side(rim)

    late_own = sweep(density, edge, *wide, LATE, LATE[0], LATE[0], 1)
    late_one = hop(late_own)
    first_own = sweep(density, after(edge, late_own), *wide, FIRST, FIRST[0], FIRST[0], 1)
    early_one_raw, back_away_raw, first_own = lax.optimization_barrier((early_one_raw, back_away_raw, first_own))

    first_edge = side(jnp.concatenate([early_one_raw[:, :, margin:], back_away_raw[:, :, margin:]], axis=0))
    back_away = sweep(back_away_raw, first_edge, *wide, BACK, 0, EARLY[1], 1)
    back_three_below = back_rest(back_away)
    early_one = sweep(early_one_raw, after(first_edge, back_away), *wide, EARLY, 0, 0, 4000000000)
    early_two = hop(early_one)
    late_one = after(late_one, early_one)
    late_two = hop(late_one)
    operator = length_operator(me, tile_pairs.T, len_band, after(len_taps.T, late_one), agg_kern)
    late_sum = prepare(operator, late_own, late_one, LATE)
    early_two = after(early_two, late_sum)
    early_rim = hop(early_two[:, tile_len - RIM :])
    back_three_below = after(back_three_below, early_two)
    back_two = unhop(back_three_below)
    back_one = unhop(back_two)
    late_two = after(late_two, back_two)
    late_rim = hop(late_two[:, tile_len - RIM :])

    early_rim = after(early_rim, late_two)
    out = finish(operator, (first_own, early_one), early_two, early_rim, EARLY, batches, None, 0, 2000000000)
    back_rim = back_three_below[:, tile_len - RIM :]
    out = finish(operator, (first_own, back_one), back_two, back_rim, BACK, batches, out, EARLY[1], 1)
    return finish(operator, (late_sum,), late_two, late_rim, LATE, batches, out, 0, 1)


def solution(mesh):
    in_specs = (P(None, "len", "wid"), P(), P(), P(), P(), P(), P())
    out_specs = P(None, "len", "wid")
    return jax.shard_map(shards, mesh=mesh, in_specs=in_specs, out_specs=out_specs, check_vma=False)
```

```python
import functools

import jax
import jax.numpy as jnp
from jax import lax
from jax.experimental import pallas as pl
from jax.experimental.pallas import tpu as pltpu
from jax.sharding import PartitionSpec as P

WBLK = 128
BETA = 0.5
RIM = 24
RING = 8
VMEM = 16 << 20


def cost(flops):
    return pl.CostEstimate(flops=flops, bytes_accessed=1, transcendentals=0)


def split(value):
    high = value.astype(jnp.bfloat16)
    return high, (value - high.astype(jnp.float32)).astype(jnp.bfloat16)


def band_of(distance, batch, band_ref, taps_ref):
    taps = taps_ref.shape[0]
    weights = [jnp.where(tap < band_ref[1, batch], taps_ref[tap, batch], 0.0) for tap in range(taps)]
    total = functools.reduce(lambda a, b: a + b, weights)
    inverse = 1.0 / jnp.full((1, distance.shape[1]), total, jnp.float32)
    matrix = jnp.zeros(distance.shape, jnp.float32)
    for tap in range(taps):
        matrix = jnp.where(distance == band_ref[0, batch] + tap, weights[tap], matrix)
    return matrix * inverse


def sweep_kernel(first, band_ref, taps_ref, field_ref, edge_ref, out_ref):
    batch = pl.program_id(0) + first
    rows = field_ref.shape[1]
    groups = field_ref.shape[2] // WBLK
    source = lax.broadcasted_iota(jnp.int32, (2 * WBLK, WBLK), 0)
    target = lax.broadcasted_iota(jnp.int32, (2 * WBLK, WBLK), 1)
    mat_high, mat_low = split(band_of(WBLK + target - source, batch, band_ref, taps_ref))
    pieces = [edge_ref[0]] + [field_ref[0, :, g * WBLK : (g + 1) * WBLK] for g in range(groups)]
    parts = [split(piece) for piece in pieces]

    def paired(which):
        pairs = [jnp.concatenate([parts[g][which], parts[g + 1][which]], axis=1) for g in range(groups)]
        return jnp.concatenate(pairs, axis=0)

    dot = functools.partial(jnp.dot, preferred_element_type=jnp.float32)
    both = dot(paired(0), jnp.concatenate([mat_high, mat_low], axis=1))
    moved = both[:, :WBLK] + both[:, WBLK:] + dot(paired(1), mat_high)
    for group in range(groups):
        out_ref[0, :, group * WBLK : (group + 1) * WBLK] = moved[group * rows : (group + 1) * rows]


def sweep(field, edge, band, taps, part, field_first, edge_first, flops=1):
    lo, hi = part
    _, rows, width = field.shape
    return pl.pallas_call(
        functools.partial(sweep_kernel, lo),
        grid_spec=pltpu.PrefetchScalarGridSpec(
            num_scalar_prefetch=2,
            grid=(hi - lo,),
            in_specs=[
                pl.BlockSpec((1, rows, width), lambda i, b, t: (i + field_first, 0, 0)),
                pl.BlockSpec((1, rows, WBLK), lambda i, b, t: (i + edge_first, 0, 0)),
            ],
            out_specs=pl.BlockSpec((1, rows, width), lambda i, b, t: (i, 0, 0)),
        ),
        out_shape=jax.ShapeDtypeStruct((hi - lo, rows, width), jnp.float32),
        compiler_params=pltpu.CompilerParams(vmem_limit_bytes=VMEM),
        cost_estimate=cost(flops),
        name="sweep",
    )(band, taps, field, edge)


def carve_kernel(early, back, margin, me_ref, field_ref, early_ref, back_ref, edge_ref):
    early_ref[...] = field_ref[early[0] : early[1]]
    back_ref[...] = field_ref[back[0] : back[1]]
    edge_ref[...] = field_ref[:, :, margin:]


def carve(me, field, early, back, margin):
    batches, rows, width = field.shape
    shapes = ((early[1] - early[0], rows, width), (back[1] - back[0], rows, width), (batches, rows, width - margin))
    whole = lambda i, m: (0, 0, 0)
    return pl.pallas_call(
        functools.partial(carve_kernel, early, back, margin),
        grid_spec=pltpu.PrefetchScalarGridSpec(
            num_scalar_prefetch=1,
            grid=(1,),
            in_specs=[pl.BlockSpec(field.shape, whole)],
            out_specs=[pl.BlockSpec(shape, whole) for shape in shapes],
        ),
        out_shape=[jax.ShapeDtypeStruct(shape, jnp.float32) for shape in shapes],
        compiler_params=pltpu.CompilerParams(vmem_limit_bytes=VMEM),
        cost_estimate=cost(1),
        name="carve",
    )(me, field)


def operator_kernel(me_ref, pair_ref, band_ref, taps_ref, own_ref, one_ref, two_ref, out_ref, turn_ref, base_ref):
    tile_len = own_ref.shape[1]
    batch = pl.program_id(0)

    @pl.when(batch == 0)
    def _():
        for below, ref in enumerate((own_ref, one_ref, two_ref)):
            present = (pair_ref[below, me_ref[0]] >= 0).astype(jnp.float32)
            turn_ref[:, below * tile_len : (below + 1) * tile_len] = ref[0].T * present
        column = lax.broadcasted_iota(jnp.int32, base_ref.shape, 1)
        row = lax.broadcasted_iota(jnp.int32, base_ref.shape, 0)
        tile_row, tile_col = row // tile_len, column // tile_len
        place_row = row % tile_len - tile_len * tile_row
        place_col = column % tile_len - tile_len * tile_col + jnp.where(tile_col == 3, tile_len - RIM, 0)
        base_ref[...] = jnp.where(me_ref[0] >= tile_col, place_row - place_col, -1)

    band_high, band_low = split(band_of(base_ref[...], batch, band_ref, taps_ref))
    turn_high, turn_low = split(turn_ref[...])
    dot = functools.partial(jnp.dot, preferred_element_type=jnp.float32)
    high, low = split(dot(turn_high, band_low) + dot(turn_low, band_high) + dot(turn_high, band_high))
    out_ref[0, :tile_len] = high
    out_ref[0, tile_len : 2 * tile_len] = band_high[:tile_len]
    out_ref[0, 2 * tile_len : 3 * tile_len] = low
    out_ref[0, 3 * tile_len :] = band_low[:tile_len]


def length_operator(me, pairs, band, taps, agg_kern):
    batches = taps.shape[1]
    tile_len = agg_kern.shape[1]
    depth = 3 * tile_len + RIM

    def pick(below):
        return pl.BlockSpec((1, tile_len, tile_len), lambda i, m, p, b, t: (jnp.maximum(p[below, m[0]], 0), 0, 0))

    return pl.pallas_call(
        operator_kernel,
        grid_spec=pltpu.PrefetchScalarGridSpec(
            num_scalar_prefetch=4,
            grid=(batches,),
            in_specs=[pick(0), pick(1), pick(2)],
            out_specs=pl.BlockSpec((1, 4 * tile_len, depth), lambda i, m, p, b, t: (i, 0, 0)),
            scratch_shapes=[
                pltpu.VMEM((tile_len, 3 * tile_len), jnp.float32),
                pltpu.VMEM((3 * tile_len, depth), jnp.int32),
            ],
        ),
        out_shape=jax.ShapeDtypeStruct((batches, 4 * tile_len, depth), jnp.bfloat16),
        compiler_params=pltpu.CompilerParams(vmem_limit_bytes=VMEM),
        cost_estimate=cost(10000000000),
        name="operator",
    )(me, pairs, band, taps, agg_kern, agg_kern, agg_kern)


def product(op_ref, columns, pieces, high_ref, low_ref):
    at = 0
    for ref in pieces:
        high, low = split(ref[0])
        high_ref[at : at + ref.shape[1]] = high
        low_ref[at : at + ref.shape[1]] = low
        at += ref.shape[1]
    half = op_ref.shape[1] // 2
    dot = functools.partial(jnp.dot, preferred_element_type=jnp.float32)
    four = dot(op_ref[0, :, columns], high_ref[:at])
    return four[:half] + four[half:] + dot(op_ref[0, :half, columns], low_ref[:at])


def prepare_kernel(op_ref, own_ref, one_ref, out_ref, high_ref, low_ref):
    rows = own_ref.shape[1]
    out_ref[0] = product(op_ref, slice(0, 2 * rows), (own_ref, one_ref), high_ref, low_ref)


def prepare(operator, own, one, part):
    lo, hi = part
    count, rows, width = one.shape
    tile = pl.BlockSpec((1, rows, width), lambda i: (i, 0, 0))
    return pl.pallas_call(
        prepare_kernel,
        grid=(count,),
        in_specs=[pl.BlockSpec((1,) + operator.shape[1:], lambda i: (i + lo, 0, 0)), tile, tile],
        out_specs=pl.BlockSpec((1, 2 * rows, width), lambda i: (i, 0, 0)),
        out_shape=jax.ShapeDtypeStruct((count, 2 * rows, width), jnp.float32),
        scratch_shapes=[pltpu.VMEM((2 * rows, width), jnp.bfloat16)] * 2,
        compiler_params=pltpu.CompilerParams(vmem_limit_bytes=VMEM),
        cost_estimate=cost(1),
        name="prepare",
    )(operator, own, one)


def update(both):
    rows = both.shape[0] // 2
    rate, spread = both[:rows], both[rows:]
    return spread + BETA * (rate * rate / (1.0 + rate) - spread * rate)


def finish_kernel(op_ref, own_ref, one_ref, two_ref, rim_ref, *rest):
    out_ref, high_ref, low_ref = rest[-3:]
    pieces = (own_ref, one_ref, two_ref, rim_ref)
    out_ref[0] = update(product(op_ref, slice(None), pieces, high_ref, low_ref))


def complete_kernel(op_ref, sum_ref, two_ref, rim_ref, *rest):
    out_ref, high_ref, low_ref = rest[-3:]
    rows = two_ref.shape[1]
    columns = slice(2 * rows, op_ref.shape[2])
    at = 0
    for ref in (two_ref, rim_ref):
        high, low = split(ref[0])
        high_ref[at : at + ref.shape[1]] = high
        low_ref[at : at + ref.shape[1]] = low
        at += ref.shape[1]
    dot = functools.partial(jnp.dot, preferred_element_type=jnp.float32)
    op_high, op_low = op_ref[0, :rows, columns], op_ref[0, 2 * rows : 3 * rows, columns]
    late = dot(op_high, high_ref[:at]) + dot(op_low, high_ref[:at]) + dot(op_high, low_ref[:at])
    rate, spread = sum_ref[0, :rows] + late, sum_ref[0, rows:]
    out_ref[0] = spread + BETA * (rate * rate / (1.0 + rate) - spread * rate)


def finish(operator, held, two, rim, part, total, before, held_first, flops):
    lo, hi = part
    count, rows, width = two.shape
    depth = operator.shape[2]
    here = lambda i: (i, 0, 0)
    firsts = (held_first, 0)
    in_specs = [pl.BlockSpec((1, operator.shape[1], depth), lambda i: (i + lo, 0, 0))]
    for first, value in zip(firsts, held):
        in_specs.append(pl.BlockSpec((1,) + value.shape[1:], lambda i, first=first: (i + first, 0, 0)))
    in_specs += [pl.BlockSpec((1, rows, width), here), pl.BlockSpec((1, RIM, width), here)]
    operands = [operator, *held, two, rim]
    aliases = {}
    if before is not None:
        aliases = {len(operands): 0}
        in_specs.append(pl.BlockSpec(memory_space=pl.ANY))
        operands.append(before)
    return pl.pallas_call(
        finish_kernel if len(held) == 2 else complete_kernel,
        grid=(count,),
        in_specs=in_specs,
        out_specs=pl.BlockSpec((1, rows, width), lambda i: (i + lo, 0, 0)),
        out_shape=jax.ShapeDtypeStruct((total, rows, width), jnp.float32),
        scratch_shapes=[pltpu.VMEM((depth, width), jnp.bfloat16)] * 2,
        input_output_aliases=aliases,
        compiler_params=pltpu.CompilerParams(vmem_limit_bytes=VMEM),
        cost_estimate=cost(flops),
        name="finish",
    )(*operands)


EARLY = (0, 6)
BACK = (6, 9)
LATE = (9, 16)
FIRST = (0, 9)


def after(value, *earlier):
    return lax.optimization_barrier((value,) + earlier)[0]


def shards(density, len_band, wid_band, len_taps, wid_taps, tile_pairs, agg_kern):
    batches, tile_len, group_width = density.shape
    tiles = lax.axis_size("len")
    groups = lax.axis_size("wid")
    margin = group_width - WBLK

    def spot(tile, step):
        return tile // RING * RING + (tile + step) % RING

    def move(pairs):
        return functools.partial(lax.ppermute, axis_name="len", perm=pairs)

    hop = move([(t, (t + 1) % tiles) for t in range(tiles)])
    unhop = move([(t, (t - 1) % tiles) for t in range(tiles)])
    back_first = move([(t, spot(t, -2)) for t in range(tiles)])
    back_rest = move([(spot(t, -2), (t + 3) % tiles) for t in range(tiles)])
    side = functools.partial(lax.ppermute, axis_name="wid", perm=[(s, s + 1) for s in range(groups - 1)])
    wide = (wid_band, wid_taps.T)

    me = lax.axis_index("len")[None].astype(jnp.int32)
    early, back, rim = carve(me, density, EARLY, BACK, margin)
    early_one_raw = hop(early)
    back_away_raw = back_first(back)
    edge = side(rim)

    late_own = sweep(density, edge, *wide, LATE, LATE[0], LATE[0], 1)
    late_one = hop(late_own)
    first_own = sweep(density, after(edge, late_own), *wide, FIRST, FIRST[0], FIRST[0], 1)
    early_one_raw, back_away_raw, first_own = lax.optimization_barrier((early_one_raw, back_away_raw, first_own))

    first_edge = side(jnp.concatenate([early_one_raw[:, :, margin:], back_away_raw[:, :, margin:]], axis=0))
    back_away = sweep(back_away_raw, first_edge, *wide, BACK, 0, EARLY[1], 1)
    back_three_below = back_rest(back_away)
    early_one = sweep(early_one_raw, after(first_edge, back_away), *wide, EARLY, 0, 0, 4000000000)
    early_two = hop(early_one)
    late_one = after(late_one, early_one)
    late_two = hop(late_one)
    operator = length_operator(me, tile_pairs.T, len_band, after(len_taps.T, late_one), agg_kern)
    late_sum = prepare(operator, late_own, late_one, LATE)
    early_two = after(early_two, late_sum)
    early_rim = hop(early_two[:, tile_len - RIM :])
    back_three_below = after(back_three_below, early_two)
    back_two = unhop(back_three_below)
    back_one = unhop(back_two)
    late_two = after(late_two, back_two)
    late_rim = hop(late_two[:, tile_len - RIM :])

    early_rim = after(early_rim, late_two)
    out = finish(operator, (first_own, early_one), early_two, early_rim, EARLY, batches, None, 0, 2000000000)
    back_rim = back_three_below[:, tile_len - RIM :]
    out = finish(operator, (first_own, back_one), back_two, back_rim, BACK, batches, out, EARLY[1], 1)
    return finish(operator, (late_sum,), late_two, late_rim, LATE, batches, out, 0, 1)


def solution(mesh):
    in_specs = (P(None, "len", "wid"), P(), P(), P(), P(), P(), P())
    out_specs = P(None, "len", "wid")
    return jax.shard_map(shards, mesh=mesh, in_specs=in_specs, out_specs=out_specs, check_vma=False)
```
